32 devices in a mesh: view: 8 (over y, x, core), band: 4 (over z).
Axes of the slice: x: 2, y: 2, z: 4, core: 2. Of those that a mesh axis runs over, the one named last changes fastest.
Arguments:
- gaussians: float32 [512, 62, 256], P(('view', 'band')), may hold values from -8 to 128, as said below
- first_moment: float32 [512, 62, 256], P(('view', 'band')), may hold values from -0.6 to 0.6
- second_moment: float32 [512, 62, 256], P(('view', 'band')), may hold values from 0.0001 to 0.1
- camera: float32 [8, 9], P('view'), may hold values from -352 to 352, as said below
- target: float32 [8, 3, 64, 128], P('view', None, 'band'), may hold values from 0 to 1
- block_list: int32 [8, 4, 16], P('view', 'band'), may hold values from -1 to 511, as said below
- block_count: int32 [8, 4], P('view', 'band'), may hold values from 12 to 16, as said below
- tile_start: int32 [8, 4, 8], P('view', 'band'), may hold values from 0 to 15, as said below
- tile_end: int32 [8, 4, 8], P('view', 'band'), may hold values from 1 to 16, as said below
Outputs:
- new_gaussians: float32 [512, 62, 256], P(('view', 'band'))
- new_first_moment: float32 [512, 62, 256], P(('view', 'band'))
- new_second_moment: float32 [512, 62, 256], P(('view', 'band'))
- mean_loss: float32 [], replicated
- grads: float32 [512, 62, 256], P(('view', 'band'))
The draws below stay inside these ranges and needn't reach their ends.
Inputs may be any that keep to these rules, and one draw needn't show every extreme that they name: Block k is held by device k // 16, devices counted with view slowest. Entry i of block_list[v, b] is a block for i < block_count[v, b] and -1 after; the live entries of one band are distinct, at most 1 of them are held by one device, and in every band some device holds exactly 1 of them. `block_count`: some band has exactly 16. tile_start < tile_end <= block_count of the band; tile_end - tile_start is at most 2, and exactly 2 for some tile of every band; the tiles of a band together cover every live position. `tile_end`: see tile_start. `gaussians`: component 9 of every Gaussian lies in [1, 2]; components 6 to 8 lie in [0, 2]. `camera`: A0 x A1 has a third entry of 0.6 or more.
All inputs are finite; a program needn't handle non-finite values.
Results may differ from the reference program's by a relative error of at most 0.0003.
Values sent between devices are 32-bit elements; how exact they have to be, the bound alone decides.
A program may use at most 128 MiB of HBM per device.

```python
import math
import jax
import jax.numpy as jnp
import numpy as np
from jax import lax

PARAMS = 62
BLOCK = 256
TILE = 16
ROWS = 16
COLS = 128
BLK_DEV = 16
LIST = 16
TILE_MOST = 2
VIEWS = 8
BANDS = 4
IMG_ROWS = 64
NBLK = 512
TILES = 8
CAP = 1
DEVICES = 32


def lists_helper(key):
    base_key = jax.random.fold_in(key, 7311)
    key_full, key_count, key_device = jax.random.split(base_key, 3)
    dev_total = VIEWS * BANDS
    slot_total = DEVICES * CAP
    counts = jax.random.randint(key_count, (dev_total,), 3 * LIST // 4, LIST + 1)
    full_device = jax.random.randint(key_full, (), 0, dev_total)
    counts = jnp.where(jnp.arange(dev_total) == full_device, LIST, counts)

    def draw_device(device_key, live_count):
        key_list = jax.random.split(device_key, 8)
        full_owner = jax.random.randint(key_list[0], (), 0, DEVICES)
        scores = jax.random.permutation(key_list[1], slot_total)
        slot_ids = jnp.arange(slot_total)
        scores = jnp.where(slot_ids // CAP == full_owner, scores - slot_total, scores)
        ranking = jnp.argsort(scores, stable=True)
        chosen = ranking[:LIST]
        half_list = LIST // 2
        front_half = chosen[:half_list][jax.random.permutation(key_list[2], half_list)]
        back_half = chosen[half_list:][jax.random.permutation(key_list[3], LIST - half_list)]
        chosen = jnp.concatenate([front_half, back_half])
        owners = chosen // CAP
        slot_rank = chosen % CAP
        local_perm = jax.vmap(lambda subkey: jax.random.permutation(subkey, BLK_DEV))(jax.random.split(key_list[4], DEVICES))
        local_ids = local_perm[owners, slot_rank]
        block_ids = owners * BLK_DEV + local_ids
        block_ids = jnp.where(jnp.arange(LIST) < live_count, block_ids, -1)
        tile_index = jnp.arange(TILES)
        low_end = tile_index * live_count // TILES
        high_end = (tile_index + 1) * live_count // TILES
        length = jax.random.randint(key_list[5], (TILES,), jnp.maximum(high_end - low_end, 1), TILE_MOST + 1)
        forced = jax.random.randint(key_list[6], (), 0, TILES)
        length = jnp.where(tile_index == forced, TILE_MOST, length)
        first_ok = jnp.maximum(0, high_end - length)
        last_ok = jnp.minimum(low_end, live_count - length)
        starts = jax.random.randint(key_list[7], (TILES,), first_ok, last_ok + 1)
        return (block_ids, starts, starts + length)
    block_ids, starts, endings = jax.vmap(draw_device)(jax.random.split(key_device, dev_total), counts)
    return (block_ids.reshape(VIEWS, BANDS, LIST).astype(jnp.int32), counts.reshape(VIEWS, BANDS).astype(jnp.int32), starts.reshape(VIEWS, BANDS, TILES).astype(jnp.int32), endings.reshape(VIEWS, BANDS, TILES).astype(jnp.int32))


def draw_block_list(key, part):
    return lists_helper(key)[0]


def draw_block_count(key, part):
    return lists_helper(key)[1]


def draw_tile_start(key, part):
    return lists_helper(key)[2]


def draw_tile_end(key, part):
    return lists_helper(key)[3]


def draw_gaussians(key, part):
    key_list = jax.random.split(jax.random.fold_in(key, 23), 8)
    grid_shape = (NBLK, BLOCK)
    extent = jnp.array([COLS * 1.0, IMG_ROWS * 1.0, 64.0], jnp.float32)[:, None, None]
    centre = jax.random.uniform(key_list[0], (3,) + grid_shape) * extent
    velocity = jnp.clip(2.0 * jax.random.normal(key_list[1], (3,) + grid_shape), -8.0, 8.0)
    log_scale = jax.random.uniform(key_list[2], (3,) + grid_shape, minval=math.log(1.2), maxval=math.log(4.0))
    quat_real = jax.random.uniform(key_list[3], (1,) + grid_shape, minval=1.0, maxval=2.0)
    quat_vec = jnp.clip(0.5 * jax.random.normal(key_list[4], (3,) + grid_shape), -2.0, 2.0)
    opacity = jax.random.uniform(key_list[5], (1,) + grid_shape, minval=-4.5, maxval=-2.5)
    sh_base = jnp.clip(0.6 * jax.random.normal(key_list[6], (3,) + grid_shape), -3.0, 3.0)
    sh_rest = jnp.clip(0.25 * jax.random.normal(key_list[7], (45,) + grid_shape), -1.5, 1.5)
    stacked = jnp.concatenate([centre, velocity, log_scale, quat_real, quat_vec, opacity, sh_base, sh_rest], axis=0)
    return stacked.transpose(1, 0, 2).astype(jnp.float32)


def draw_camera(key, part):
    key_list = jax.random.split(jax.random.fold_in(key, 41), 5)
    tilt_range = 0.3
    spin_angle = jax.random.uniform(key_list[0], (VIEWS,), minval=-0.15, maxval=0.15)
    tilt_a = jax.random.uniform(key_list[1], (VIEWS,), minval=-tilt_range, maxval=tilt_range)
    tilt_b = jax.random.uniform(key_list[2], (VIEWS,), minval=-tilt_range, maxval=tilt_range)
    zoom_factor = jax.random.uniform(key_list[3], (VIEWS,), minval=0.9, maxval=1.1)
    view_time = jax.random.uniform(key_list[4], (VIEWS,))
    row_top = zoom_factor[:, None] * jnp.stack([jnp.cos(spin_angle), -jnp.sin(spin_angle), tilt_a], axis=1)
    row_low = zoom_factor[:, None] * jnp.stack([jnp.sin(spin_angle), jnp.cos(spin_angle), tilt_b], axis=1)
    centre = jnp.array([COLS * 0.5, IMG_ROWS * 0.5, 32.0], jnp.float32)
    off_top = COLS * 0.5 - jnp.sum(row_top * centre[None, :], axis=1)
    off_low = IMG_ROWS * 0.5 - jnp.sum(row_low * centre[None, :], axis=1)
    return jnp.concatenate([row_top, row_low, off_top[:, None], off_low[:, None], view_time[:, None]], axis=1).astype(jnp.float32)


def block_scale(key, shape, pieces, low, top_value):
    loudness = 1.0
    for axis_at, blocks in pieces:
        heights = jax.random.uniform(jax.random.fold_in(jax.random.fold_in(key, 6), axis_at), (blocks,), jnp.float32, low / len(pieces), top_value / len(pieces))
        loudness = loudness * jnp.repeat(jnp.exp(heights), shape[axis_at] // blocks).reshape((-1,) + (1,) * (len(shape) - 1 - axis_at))
    return loudness


def noise(rng, shape, scale, reach, shards=(), held_as=jnp.bfloat16):
    entries = jax.random.normal(rng, shape, jnp.float32) * scale
    if len(shards) > 0:
        entries = block_scale(rng, shape, shards, -0.22, 0.18) * entries
    return jnp.clip(entries, min=-reach, max=reach).astype(held_as)


def setup_inputs(seed: int = 0) -> dict:
    key_of = jax.random.split(jax.random.key(seed), 10)
    return {
        "gaussians": draw_gaussians(jax.random.fold_in(key_of[9], 71), 0),
        "first_moment": noise(key_of[1], (NBLK, PARAMS, BLOCK), 0.1, 0.6, ((0, 32),), jnp.float32),
        "second_moment": jnp.clip(jnp.exp(math.log(0.1) - 6.9077553 * jax.random.uniform(key_of[2], (NBLK, PARAMS, BLOCK), jnp.float32) ** block_scale(key_of[2], (NBLK, PARAMS, BLOCK), ((0, 32),), -0.2, 0.2)), 0.0001, 0.1),
        "camera": draw_camera(jax.random.fold_in(key_of[9], 71), 0),
        "target": jnp.clip(1.0 * jax.random.uniform(key_of[4], (VIEWS, 3, IMG_ROWS, COLS), jnp.float32) ** block_scale(key_of[4], (VIEWS, 3, IMG_ROWS, COLS), ((0, 8), (2, 4)), -0.2, 0.2), 0.0, 1.0),
        "block_list": draw_block_list(jax.random.fold_in(key_of[9], 71), 0),
        "block_count": draw_block_count(jax.random.fold_in(key_of[9], 71), 0),
        "tile_start": draw_tile_start(jax.random.fold_in(key_of[9], 71), 0),
        "tile_end": draw_tile_end(jax.random.fold_in(key_of[9], 71), 0),
    }


HIGHEST_MODE = lax.Precision.HIGHEST
SSIM_WEIGHT = 0.2
ABS_WEIGHT = 0.8
STAB_MEAN = 0.0001
STAB_VAR = 0.0009
BIAS_FIRST = 1.0 - math.exp(100.0 * math.log(0.9))
BIAS_SECOND = 1.0 - math.exp(100.0 * math.log(0.999))
SH_ZERO = 0.28209479177387814
SH_ONE = 0.4886025119029199
SH_TWO = [1.0925484305920792, -1.0925484305920792, 0.31539156525252005, -1.0925484305920792, 0.5462742152960396]
SH_THREE = [-0.5900435899266435, 2.890611442640554, -0.4570457994644658, 0.3731763325901154, -0.4570457994644658, 1.445305721320277, -0.5900435899266435]

def learning_rates():
    return np.concatenate([np.full(6, 0.016), np.full(3, 0.005), np.full(4, 0.001), np.full(1, 0.05), np.full(3, 0.0025), np.full(45, 0.000125)]).astype(np.float32)

def kernel_taps():
    raw_taps = [math.exp(-(offset * offset) / 4.5) for offset in range(-5, 6)]
    tap_total = sum(raw_taps)
    return [raw_tap / tap_total for raw_tap in raw_taps]

def smooth(source, rows_out):
    kernel = kernel_taps()
    rows_done = kernel[0] * source[..., 0:rows_out, :]
    for offset in range(1, 11):
        rows_done = rows_done + kernel[offset] * source[..., offset:offset + rows_out, :]
    cols_n = source.shape[-1]
    padded = jnp.pad(rows_done, [(0, 0)] * (source.ndim - 1) + [(5, 5)])
    result = kernel[0] * padded[..., 0:cols_n]
    for offset in range(1, 11):
        result = result + kernel[offset] * padded[..., offset:offset + cols_n]
    return result

def ssim_value(mean_x, mean_y, square_x, square_y, cross_xy):
    var_x = square_x - mean_x * mean_x
    var_y = square_y - mean_y * mean_y
    covar = cross_xy - mean_x * mean_y
    upper = (2.0 * mean_x * mean_y + STAB_MEAN) * (2.0 * covar + STAB_VAR)
    lower = (mean_x * mean_x + mean_y * mean_y + STAB_MEAN) * (var_x + var_y + STAB_VAR)
    return upper / lower

def ssim_terms(pred_ext, target_ext, rows_out):
    mean_x = smooth(pred_ext, rows_out)
    mean_y = smooth(target_ext, rows_out)
    square_x = smooth(pred_ext * pred_ext, rows_out)
    square_y = smooth(target_ext * target_ext, rows_out)
    cross_xy = smooth(pred_ext * target_ext, rows_out)
    ssim_map, pullback = jax.vjp(ssim_value, mean_x, mean_y, square_x, square_y, cross_xy)
    partials = pullback(jnp.full_like(ssim_map, -SSIM_WEIGHT / 3.0))
    return (ssim_map, partials[0], partials[2], partials[4])

def harmonics(facing):
    dir_x, dir_y, dir_z = (facing[0], facing[1], facing[2])
    sq_x, sq_y, sq_z = (dir_x * dir_x, dir_y * dir_y, dir_z * dir_z)
    return jnp.stack([SH_ZERO + 0.0 * dir_x, -SH_ONE * dir_y, SH_ONE * dir_z, -SH_ONE * dir_x, SH_TWO[0] * dir_x * dir_y, SH_TWO[1] * dir_y * dir_z, SH_TWO[2] * (2.0 * sq_z - sq_x - sq_y), SH_TWO[3] * dir_x * dir_z, SH_TWO[4] * (sq_x - sq_y), SH_THREE[0] * dir_y * (3.0 * sq_x - sq_y), SH_THREE[1] * dir_x * dir_y * dir_z, SH_THREE[2] * dir_y * (4.0 * sq_z - sq_x - sq_y), SH_THREE[3] * dir_z * (2.0 * sq_z - 3.0 * sq_x - 3.0 * sq_y), SH_THREE[4] * dir_x * (4.0 * sq_z - sq_x - sq_y), SH_THREE[5] * dir_z * (sq_x - sq_y), SH_THREE[6] * dir_x * (sq_x - 3.0 * sq_y)])

def project(window, cam_row):
    affine = cam_row[0:6].reshape(2, 3)
    cam_time = cam_row[8]
    centre = [window[:, axis_k, :] + cam_time * window[:, 3 + axis_k, :] for axis_k in range(3)]
    col_pos = affine[0, 0] * centre[0] + affine[0, 1] * centre[1] + affine[0, 2] * centre[2] + cam_row[6]
    row_pos = affine[1, 0] * centre[0] + affine[1, 1] * centre[1] + affine[1, 2] * centre[2] + cam_row[7]
    scales = [jnp.exp(window[:, 6 + axis_k, :]) for axis_k in range(3)]
    quat_len = jnp.sqrt(window[:, 9, :] * window[:, 9, :] + window[:, 10, :] * window[:, 10, :] + window[:, 11, :] * window[:, 11, :] + window[:, 12, :] * window[:, 12, :])
    quat_r = window[:, 9, :] / quat_len
    quat_i = window[:, 10, :] / quat_len
    quat_j = window[:, 11, :] / quat_len
    quat_k = window[:, 12, :] / quat_len
    rotation = [[1.0 - 2.0 * (quat_j * quat_j + quat_k * quat_k), 2.0 * (quat_i * quat_j - quat_r * quat_k), 2.0 * (quat_i * quat_k + quat_r * quat_j)], [2.0 * (quat_i * quat_j + quat_r * quat_k), 1.0 - 2.0 * (quat_i * quat_i + quat_k * quat_k), 2.0 * (quat_j * quat_k - quat_r * quat_i)], [2.0 * (quat_i * quat_k - quat_r * quat_j), 2.0 * (quat_j * quat_k + quat_r * quat_i), 1.0 - 2.0 * (quat_i * quat_i + quat_j * quat_j)]]
    spread_rows = [[(affine[out_row, 0] * rotation[0][in_col] + affine[out_row, 1] * rotation[1][in_col] + affine[out_row, 2] * rotation[2][in_col]) * scales[in_col] for in_col in range(3)] for out_row in range(2)]
    conic_a = spread_rows[0][0] * spread_rows[0][0] + spread_rows[0][1] * spread_rows[0][1] + spread_rows[0][2] * spread_rows[0][2] + 0.3
    conic_b = spread_rows[0][0] * spread_rows[1][0] + spread_rows[0][1] * spread_rows[1][1] + spread_rows[0][2] * spread_rows[1][2]
    conic_c = spread_rows[1][0] * spread_rows[1][0] + spread_rows[1][1] * spread_rows[1][1] + spread_rows[1][2] * spread_rows[1][2] + 0.3
    determinant = conic_a * conic_c - conic_b * conic_b
    opacity = jax.nn.sigmoid(window[:, 13, :])
    normal = jnp.cross(affine[0], affine[1])
    facing = normal / jnp.sqrt(jnp.sum(normal * normal))
    sh_basis = harmonics(facing)
    sh_coef = window[:, 14:, :].reshape(window.shape[0], 16, 3, window.shape[2])
    colour = 0.5 + jnp.einsum('k,tkcb->ctb', sh_basis, sh_coef, precision=HIGHEST_MODE)
    return (col_pos, row_pos, conic_a, conic_b, conic_c, determinant, opacity, colour)

def render_tile(window, cam_row, first_pos, live_low, live_high, row_start, col_start):
    window_len = window.shape[0]
    block_len = window.shape[2]
    col_pos, row_pos, conic_a, conic_b, conic_c, determinant, opacity, colour = project(window, cam_row)
    positions = first_pos + jnp.arange(window_len, dtype=jnp.int32)
    is_live = (positions >= live_low) & (positions < live_high)
    live_flat = jnp.repeat(is_live, block_len)
    pixels = jnp.arange(TILE * TILE, dtype=jnp.int32)
    pix_row = (row_start + pixels // TILE).astype(jnp.float32) + 0.5
    pix_col = (col_start + pixels % TILE).astype(jnp.float32) + 0.5
    delta_col = pix_col[None, :] - col_pos.reshape(-1)[:, None]
    delta_row = pix_row[None, :] - row_pos.reshape(-1)[:, None]
    exponent = -0.5 * (conic_c.reshape(-1)[:, None] * delta_col * delta_col - 2.0 * conic_b.reshape(-1)[:, None] * delta_col * delta_row + conic_a.reshape(-1)[:, None] * delta_row * delta_row) / determinant.reshape(-1)[:, None]
    alphas = jnp.where(live_flat[:, None], opacity.reshape(-1)[:, None] * jnp.exp(exponent), 0.0)
    keep_log = jnp.log1p(-alphas).reshape(window_len, block_len, -1)
    inner_sum = jnp.cumsum(keep_log, axis=1)
    block_total = inner_sum[:, -1, :]
    outer_sum = jnp.cumsum(block_total, axis=0) - block_total
    log_trans = inner_sum - keep_log + outer_sum[:, None, :]
    weight = alphas * jnp.exp(log_trans.reshape(window_len * block_len, -1))
    return jnp.dot(colour.reshape(3, -1), weight, precision=HIGHEST_MODE)

def tile_frame(tile_index, starts, list_len, row_base):
    tile_cols = COLS // TILE
    first_pos = jnp.minimum(starts[tile_index], list_len - TILE_MOST).astype(jnp.int32)
    row_start = row_base + tile_index // tile_cols * TILE
    col_start = tile_index % tile_cols * TILE
    return (first_pos, row_start, col_start)

def from_tiles(tiles_out):
    tile_rows = ROWS // TILE
    tile_cols = COLS // TILE
    return tiles_out.reshape(tile_rows, tile_cols, 3, TILE, TILE).transpose(2, 0, 3, 1, 4).reshape(3, ROWS, COLS)

def to_tiles(image):
    tile_rows = ROWS // TILE
    tile_cols = COLS // TILE
    return image.reshape(3, tile_rows, TILE, tile_cols, TILE).transpose(1, 3, 0, 2, 4).reshape(tile_rows * tile_cols, 3, TILE * TILE)

def render_band(listed, cam_row, starts, endings, row_base):
    list_len = listed.shape[0]

    def draw_tile(tile_index):
        first_pos, row_start, col_start = tile_frame(tile_index, starts, list_len, row_base)
        window = lax.dynamic_slice_in_dim(listed, first_pos, TILE_MOST, 0)
        return render_tile(window, cam_row, first_pos, starts[tile_index], endings[tile_index], row_start, col_start)
    tiles_out = lax.map(draw_tile, jnp.arange(starts.shape[0], dtype=jnp.int32))
    return from_tiles(tiles_out)

def backward_band(listed, cam_row, starts, endings, row_base, grad_pred):
    list_len = listed.shape[0]
    cot_tiles = to_tiles(grad_pred)

    def tile_back(summed, tile_index):
        first_pos, row_start, col_start = tile_frame(tile_index, starts, list_len, row_base)
        window = lax.dynamic_slice_in_dim(listed, first_pos, TILE_MOST, 0)

        def draw_window(chosen):
            return render_tile(chosen, cam_row, first_pos, starts[tile_index], endings[tile_index], row_start, col_start)
        unused, pullback = jax.vjp(draw_window, window)
        grad_window = pullback(cot_tiles[tile_index])[0]
        current = lax.dynamic_slice_in_dim(summed, first_pos, TILE_MOST, 0)
        summed = lax.dynamic_update_slice_in_dim(summed, current + grad_window, first_pos, 0)
        return (summed, None)
    summed, unused = lax.scan(tile_back, jnp.zeros_like(listed), jnp.arange(starts.shape[0], dtype=jnp.int32))
    return summed

def image_loss(pred_img, target_img):
    pad_rows = [(0, 0), (5, 5), (0, 0)]
    ssim_map, part_mean, part_square, part_cross = ssim_terms(jnp.pad(pred_img, pad_rows), jnp.pad(target_img, pad_rows), IMG_ROWS)
    adjoint = jnp.pad(jnp.stack([part_mean, part_square, part_cross]), [(0, 0), (0, 0), (5, 5), (0, 0)])
    spread = smooth(adjoint, IMG_ROWS)
    error_map = pred_img - target_img
    grad_pred = ABS_WEIGHT / 3.0 * jnp.sign(error_map) + spread[0] + 2.0 * pred_img * spread[1] + target_img * spread[2]
    summed = jnp.sum(ABS_WEIGHT / 3.0 * jnp.abs(error_map) + SSIM_WEIGHT / 3.0 * (1.0 - ssim_map))
    return (summed, grad_pred)

def adam_update(params, moment_one, moment_two, gradient):
    learn_rates = jnp.asarray(learning_rates())[None, :, None]
    new_one = 0.9 * moment_one + 0.1 * gradient
    new_two = 0.999 * moment_two + 0.001 * gradient * gradient
    change = learn_rates * (new_one / BIAS_FIRST) / (jnp.sqrt(new_two / BIAS_SECOND) + 1e-08)
    return (params - change, new_one, new_two)

def reference(gaussians, first_moment, second_moment, camera, target, block_list, block_count, tile_start, tile_end):
    nblk_total = gaussians.shape[0]
    list_len = block_list.shape[2]
    dev_total = VIEWS * BANDS
    list_rows = block_list.reshape(dev_total, list_len)
    counts = block_count.reshape(dev_total)
    starts = tile_start.reshape(dev_total, -1)
    endings = tile_end.reshape(dev_total, -1)
    position = jnp.arange(list_len, dtype=jnp.int32)

    def fetch(device):
        safe_ids = jnp.where(position < counts[device], list_rows[device], 0).astype(jnp.int32)
        return jnp.take(gaussians, safe_ids, axis=0)

    def render_device(device):
        view_index = device // BANDS
        band_index = device % BANDS
        return render_band(fetch(device), camera[view_index], starts[device], endings[device], band_index * ROWS)
    rendered = lax.map(render_device, jnp.arange(dev_total, dtype=jnp.int32))
    images = rendered.reshape(VIEWS, BANDS, 3, ROWS, COLS).transpose(0, 2, 1, 3, 4).reshape(VIEWS, 3, IMG_ROWS, COLS)
    totals, grad_images = jax.vmap(image_loss)(images, target)
    mean_loss = jnp.sum(totals) / (VIEWS * IMG_ROWS * COLS)
    grad_bands = grad_images.reshape(VIEWS, 3, BANDS, ROWS, COLS).transpose(0, 2, 1, 3, 4).reshape(dev_total, 3, ROWS, COLS)

    def accumulate(summed, device):
        view_index = device // BANDS
        band_index = device % BANDS
        grads_list = backward_band(fetch(device), camera[view_index], starts[device], endings[device], band_index * ROWS, grad_bands[device])
        target_rows = jnp.where(position < counts[device], list_rows[device], nblk_total).astype(jnp.int32)
        summed = summed.at[target_rows].add(grads_list, mode='drop')
        return (summed, None)
    gradient, unused = lax.scan(accumulate, jnp.zeros_like(gaussians), jnp.arange(dev_total, dtype=jnp.int32))
    new_params, new_one, new_two = adam_update(gaussians, first_moment, second_moment, gradient)
    return (new_params, new_one, new_two, mean_loss, gradient)
```

```python
import functools
import math

import jax
import jax.numpy as jnp
import numpy as np
from jax import lax
from jax.experimental import pallas as pl
from jax.experimental.pallas import tpu as pltpu
from jax.sharding import PartitionSpec as P

TILE = 16
TILE_MOST = 2
HALO = 5
REACH = 2 * HALO
ROW_REC = 9

HIGHEST_MODE = lax.Precision.HIGHEST
SSIM_WEIGHT = 0.2
ABS_WEIGHT = 0.8
STAB_MEAN = 0.0001
STAB_VAR = 0.0009
BIAS_FIRST = 1.0 - math.exp(100.0 * math.log(0.9))
BIAS_SECOND = 1.0 - math.exp(100.0 * math.log(0.999))
LOG2_E = math.log2(math.e)
SH_ZERO = 0.28209479177387814
SH_ONE = 0.4886025119029199
SH_TWO = [
    1.0925484305920792,
    -1.0925484305920792,
    0.31539156525252005,
    -1.0925484305920792,
    0.5462742152960396,
]
SH_THREE = [
    -0.5900435899266435,
    2.890611442640554,
    -0.4570457994644658,
    0.3731763325901154,
    -0.4570457994644658,
    1.445305721320277,
    -0.5900435899266435,
]
F32 = jnp.float32
BF16 = jnp.bfloat16
MESH = pl.DeviceIdType.MESH
NEVER = -1e30


def learning_rates():
    return np.concatenate(
        [
            np.full(6, 0.016),
            np.full(3, 0.005),
            np.full(4, 0.001),
            np.full(1, 0.05),
            np.full(3, 0.0025),
            np.full(45, 0.000125),
        ]
    ).astype(np.float32)


def kernel_taps():
    raw_taps = [math.exp(-(offset * offset) / 4.5) for offset in range(-5, 6)]
    tap_total = sum(raw_taps)
    return [raw_tap / tap_total for raw_tap in raw_taps]


def up8(value):
    return (value + 7) // 8 * 8


def smoothing_tables(rows, cols, channels):
    taps = kernel_taps()
    in_rows, mid_rows = up8(rows + 2 * REACH), up8(rows + REACH)
    across = np.zeros((cols, cols), np.float32)
    for out in range(cols):
        for m in range(-HALO, HALO + 1):
            if 0 <= out + m < cols:
                across[out + m, out] = taps[m + HALO]
    first = np.zeros((channels * mid_rows, channels * in_rows), np.float32)
    second = np.zeros((channels * rows, channels * mid_rows), np.float32)
    for c in range(channels):
        for e in range(rows + REACH):
            for m in range(REACH + 1):
                first[c * mid_rows + e, c * in_rows + e + m] = taps[m]
        for i in range(rows):
            for m in range(REACH + 1):
                second[c * rows + i, c * mid_rows + i + m] = taps[m]
    return across, first, second


def power_table(tiles, cols):
    lane = np.arange(cols)
    local = lane % TILE + 0.5 - TILE / 2
    belongs = (lane[None, :] // TILE == np.arange(tiles)[:, None]).astype(np.float32)
    return np.concatenate([belongs, belongs * local, belongs * local * local]).astype(np.float32)


def harmonics(dir_x, dir_y, dir_z):
    sq_x, sq_y, sq_z = (dir_x * dir_x, dir_y * dir_y, dir_z * dir_z)
    return [
        SH_ZERO + 0.0 * dir_x,
        -SH_ONE * dir_y,
        SH_ONE * dir_z,
        -SH_ONE * dir_x,
        SH_TWO[0] * dir_x * dir_y,
        SH_TWO[1] * dir_y * dir_z,
        SH_TWO[2] * (2.0 * sq_z - sq_x - sq_y),
        SH_TWO[3] * dir_x * dir_z,
        SH_TWO[4] * (sq_x - sq_y),
        SH_THREE[0] * dir_y * (3.0 * sq_x - sq_y),
        SH_THREE[1] * dir_x * dir_y * dir_z,
        SH_THREE[2] * dir_y * (4.0 * sq_z - sq_x - sq_y),
        SH_THREE[3] * dir_z * (2.0 * sq_z - 3.0 * sq_x - 3.0 * sq_y),
        SH_THREE[4] * dir_x * (4.0 * sq_z - sq_x - sq_y),
        SH_THREE[5] * dir_z * (sq_x - sq_y),
        SH_THREE[6] * dir_x * (sq_x - 3.0 * sq_y),
    ]


def camera_basis(affine):
    a, b = affine[0:3], affine[3:6]
    n_x = a[1] * b[2] - a[2] * b[1]
    n_y = a[2] * b[0] - a[0] * b[2]
    n_z = a[0] * b[1] - a[1] * b[0]
    length = jnp.sqrt(n_x * n_x + n_y * n_y + n_z * n_z)
    return harmonics(n_x / length, n_y / length, n_z / length)


def shape_of(affine, logs, quats, logit):
    scales = [jnp.exp(value) for value in logs]
    quat_len = jnp.sqrt(
        quats[0] * quats[0] + quats[1] * quats[1] + quats[2] * quats[2] + quats[3] * quats[3]
    )
    r, i, j, k = [value / quat_len for value in quats]
    rotation = [
        [1.0 - 2.0 * (j * j + k * k), 2.0 * (i * j - r * k), 2.0 * (i * k + r * j)],
        [2.0 * (i * j + r * k), 1.0 - 2.0 * (i * i + k * k), 2.0 * (j * k - r * i)],
        [2.0 * (i * k - r * j), 2.0 * (j * k + r * i), 1.0 - 2.0 * (i * i + j * j)],
    ]
    m = [
        [
            (
                affine[3 * o] * rotation[0][c]
                + affine[3 * o + 1] * rotation[1][c]
                + affine[3 * o + 2] * rotation[2][c]
            )
            * scales[c]
            for c in range(3)
        ]
        for o in range(2)
    ]
    conic_a = m[0][0] * m[0][0] + m[0][1] * m[0][1] + m[0][2] * m[0][2] + 0.3
    conic_b = m[0][0] * m[1][0] + m[0][1] * m[1][1] + m[0][2] * m[1][2]
    conic_c = m[1][0] * m[1][0] + m[1][1] * m[1][1] + m[1][2] * m[1][2] + 0.3
    opacity = 1.0 / (1.0 + jnp.exp(-logit))
    return conic_a, conic_b, conic_c, opacity


def split3(value, axis=0):
    high = value.astype(BF16)
    rest = value - high.astype(F32)
    middle = rest.astype(BF16)
    low = (rest - middle.astype(F32)).astype(BF16)
    return high, middle, low


def exact_dot(table, value, dims):
    table = table.astype(BF16)
    total = None
    for part in split3(value):
        term = lax.dot_general(table, part, (dims, ((), ())), preferred_element_type=F32)
        total = term if total is None else total + term
    return total


def expand_dot(value, table):
    table = table.astype(BF16)
    total = None
    for part in split3(value):
        term = lax.dot_general(
            part, table, (((0,), (0,)), ((), ())), preferred_element_type=F32
        )
        total = term if total is None else total + term
    return total


NN = ((1,), (0,))
NT = ((1,), (1,))


def requests_of(messages, base, list_len, blocks):
    devices = messages.shape[0]
    block_iota = lax.broadcasted_iota(jnp.int32, (devices, blocks), 1).astype(F32) + base
    hit = jnp.zeros((devices, blocks), F32)
    for i in range(list_len):
        wanted = messages[:, 16 + i : 17 + i]
        hit = hit + jnp.where(wanted == block_iota, 1.0, 0.0)
    return hit


def tree_sum(vregs, lane_count):
    sub = lax.broadcasted_iota(jnp.int32, (8, lane_count), 0)

    def join(a, b, mask, shift):
        return jnp.where(mask, a, b) + pltpu.roll(jnp.where(mask, b, a), 8 - shift, 0)

    def half(offset):
        return ((sub + (8 - offset)) % 8) < 4

    def quarter(offset):
        return ((sub + (8 - offset)) % 4) < 2

    z1 = join(
        join(vregs[0], vregs[4], half(0), 4), join(vregs[2], vregs[6], half(2), 4), quarter(0), 2
    )
    z2 = join(
        join(vregs[1], vregs[5], half(1), 4), join(vregs[3], vregs[7], half(3), 4), quarter(1), 2
    )
    return join(z1, z2, (sub % 2) < 1, 1)


def step_kernel(
    geometry,
    table_ref,
    target_ref,
    gauss_ref,
    across_ref,
    first_ref,
    second_ref,
    power_ref,
    incoming_ref,
    messages_ref,
    msg_in,
    rec_out,
    rec_in,
    grad_out,
    grad_in,
    halo_out,
    halo_in,
    thalo_out,
    thalo_in,
    coef,
    alpha_s,
    trans_s,
    moment_s,
    send_sem,
    recv_sem,
    halo_send,
    halo_recv,
):
    views_n, bands_n, blocks, list_len, rows, cols, block_len = geometry
    devices = views_n * bands_n
    tiles = cols // TILE
    pairs = TILE_MOST * tiles
    window = TILE_MOST * block_len
    halves = block_len // 128
    view = lax.axis_index("view")
    band = lax.axis_index("band")
    me = view * bands_n + band
    base = (me * blocks).astype(F32)
    has_up = band > 0
    has_down = band < bands_n - 1

    def peer_of(d):
        peer = lax.rem(me + d, devices)
        return (peer // bands_n, lax.rem(peer, bands_n))

    halo_in[...] = jnp.zeros_like(halo_in)
    thalo_in[...] = jnp.zeros_like(thalo_in)
    thalo_out[0] = target_ref[0, :, 0:REACH, :]
    thalo_out[1] = target_ref[0, :, rows - REACH : rows, :]
    barrier = pltpu.get_barrier_semaphore()

    def greet(d, carry):
        pl.semaphore_signal(barrier, inc=1, device_id=peer_of(d), device_id_type=MESH)
        return carry

    lax.fori_loop(1, devices, greet, 0)
    pl.semaphore_wait(barrier, devices - 1)

    def to_all(source_of, landing, phase):
        def send(d, carry):
            peer = lax.rem(me + d, devices)
            pltpu.make_async_remote_copy(
                src_ref=source_of(peer),
                dst_ref=landing.at[me],
                send_sem=send_sem.at[phase],
                recv_sem=recv_sem.at[phase],
                device_id=peer_of(d),
                device_id_type=MESH,
            ).start()
            return carry

        lax.fori_loop(1, devices, send, 0)

    def wait_all(landing, phase):
        every = landing.at[pl.ds(0, devices - 1)]
        pltpu.make_async_copy(every, every, recv_sem.at[phase]).wait()
        pltpu.make_async_copy(every, every, send_sem.at[phase]).wait()

    def edge_copy(source, landing, direction, phase):
        step = -1 if direction == 0 else 1
        return pltpu.make_async_remote_copy(
            src_ref=source.at[direction],
            dst_ref=landing.at[1 - direction],
            send_sem=halo_send.at[phase, direction],
            recv_sem=halo_recv.at[phase, 1 - direction],
            device_id=(view, band + step),
            device_id_type=MESH,
        )

    def edges_start(source, landing, phase):
        @pl.when(has_up)
        def _():
            edge_copy(source, landing, 0, phase).start()

        @pl.when(has_down)
        def _():
            edge_copy(source, landing, 1, phase).start()

    def edges_wait(source, landing, phase):
        @pl.when(has_up)
        def _():
            up = edge_copy(source, landing, 0, phase)
            up.wait_send()
            pltpu.make_async_copy(
                landing.at[0], landing.at[0], halo_recv.at[phase, 0]
            ).wait()

        @pl.when(has_down)
        def _():
            down = edge_copy(source, landing, 1, phase)
            down.wait_send()
            pltpu.make_async_copy(
                landing.at[1], landing.at[1], halo_recv.at[phase, 1]
            ).wait()

    message = table_ref.at[0]
    to_all(lambda peer: message, msg_in, 0)
    edges_start(thalo_out, thalo_in, 0)
    msg_in[me] = table_ref[0]

    list_row = table_ref[0][:, 16 : 16 + list_len]
    owner_low = lax.broadcasted_iota(jnp.int32, (devices, list_len), 0).astype(F32) * blocks
    owner_hot = jnp.where((list_row >= owner_low) & (list_row < owner_low + blocks), 1.0, 0.0)
    place = jnp.concatenate(
        [table_ref[1 + pair][:, 0:list_len] for pair in range(pairs)], axis=0
    )
    live_pair = jnp.max(place, axis=1, keepdims=True)
    pick_owner = lax.dot_general(
        place.astype(BF16), owner_hot.astype(BF16), (NT, ((), ())), preferred_element_type=F32
    )
    put_owner = lax.dot_general(
        owner_hot.astype(BF16), place.astype(BF16), (NT, ((), ())), preferred_element_type=F32
    )
    live = jnp.concatenate(
        [
            jnp.broadcast_to(live_pair[k * tiles : (k + 1) * tiles], (tiles, block_len))
            for k in range(TILE_MOST)
        ],
        axis=1,
    )

    wait_all(msg_in, 0)

    asked = msg_in[...].reshape(devices, 128)
    messages_ref[...] = asked
    hot = requests_of(asked, base, list_len, blocks)
    missing = 1.0 - jnp.max(hot, axis=1, keepdims=True)
    cam = [asked[:, c : c + 1] for c in range(9)]

    def picked(component):
        return exact_dot(hot, gauss_ref[:, component, :], NN)

    centre = [picked(c) + cam[8] * picked(3 + c) for c in range(3)]
    records = [
        cam[0] * centre[0] + cam[1] * centre[1] + cam[2] * centre[2] + cam[6],
        cam[3] * centre[0] + cam[4] * centre[1] + cam[5] * centre[2] + cam[7],
    ]
    quats = [picked(9 + c) for c in range(4)]
    quats[0] = quats[0] + missing
    conic_a, conic_b, conic_c, opacity = shape_of(
        cam[0:6], [picked(6 + c) for c in range(3)], quats, picked(13)
    )
    records += [conic_a, conic_b, conic_c, opacity]
    basis = camera_basis(cam)
    basis = [jnp.where(missing > 0.5, 0.0, value) for value in basis]
    for ch in range(3):
        colour = 0.5
        for q in range(16):
            colour = colour + basis[q] * picked(14 + 3 * q + ch)
        records.append(colour)
    for p in range(ROW_REC):
        for h in range(halves):
            rec_out[:, p * halves + h, :] = records[p][:, h * 128 : (h + 1) * 128]
    to_all(lambda peer: rec_out.at[peer], rec_in, 1)
    rec_in[me] = rec_out[me]
    wait_all(rec_in, 1)

    def gathered(p):
        parts = []
        for h in range(halves):
            parts.append(exact_dot(pick_owner, rec_in[:, p * halves + h, :], NN))
        whole = jnp.concatenate(parts, axis=1)
        return jnp.concatenate(
            [whole[k * tiles : (k + 1) * tiles] for k in range(TILE_MOST)], axis=1
        )

    dead = 1.0 - live
    tile_row = lax.broadcasted_iota(jnp.int32, (tiles, window), 0).astype(F32)
    u_rel = gathered(0) - (tile_row * TILE + 0.5 * TILE)
    w_rel = gathered(1) - ((band * rows).astype(F32) + 0.5 * TILE)
    c_a = gathered(2) + dead
    c_b = gathered(3)
    c_c = gathered(4) + dead
    opac = gathered(5) + dead
    inv_det = 1.0 / (c_a * c_c - c_b * c_b)
    coef_a = -0.5 * c_c * inv_det
    coef_b = c_b * inv_det
    coef_c = -0.5 * c_a * inv_det
    keep = live > 0.5

    def masked(value, other=0.0):
        return jnp.where(keep, value, other)

    flat = LOG2_E * (
        coef_a * u_rel * u_rel + coef_b * u_rel * w_rel + coef_c * w_rel * w_rel
    ) + LOG2_E * jnp.log(opac)
    power = power_ref[...]
    coef[0] = expand_dot(
        jnp.concatenate(
            [
                masked(flat, NEVER),
                masked(LOG2_E * (-2.0 * coef_a * u_rel - coef_b * w_rel)),
                masked(LOG2_E * coef_a),
            ],
            axis=0,
        ),
        power,
    )
    coef[1] = expand_dot(
        jnp.concatenate(
            [
                masked(LOG2_E * (-coef_b * u_rel - 2.0 * coef_c * w_rel)),
                masked(LOG2_E * coef_b),
            ],
            axis=0,
        ),
        power[0 : 2 * tiles],
    )
    coef[2] = expand_dot(masked(LOG2_E * coef_c), power[0:tiles])
    for ch in range(3):
        coef[3 + ch] = expand_dot(masked(gathered(6 + ch)), power[0:tiles])

    sub8 = lax.broadcasted_iota(jnp.int32, (8, cols), 0).astype(F32)
    parts_n = rows // 8
    row_local = [sub8 + (8.0 * part + 0.5 - 0.5 * TILE) for part in range(parts_n)]

    def spread_row(kind, j):
        return coef[kind, pl.ds(j, 8, stride=0), :]

    def blend(group, carry):
        trans, image = carry
        trans, image = list(trans), list(image)
        for k in range(8):
            j = group * 8 + k
            q0, q1, q2 = spread_row(0, j), spread_row(1, j), spread_row(2, j)
            tint = [spread_row(3 + ch, j) for ch in range(3)]
            for part in range(parts_n):
                r = row_local[part]
                alpha = jnp.exp2(q0 + r * (q1 + r * q2))
                weight = alpha * trans[part]
                alpha_s[j, part] = alpha
                trans_s[j, part] = trans[part]
                trans[part] = trans[part] - weight
                for ch in range(3):
                    at = ch * parts_n + part
                    image[at] = image[at] + weight * tint[ch]
        return tuple(trans), tuple(image)

    zero = jnp.zeros((8, cols), F32)
    _, image = lax.fori_loop(
        0,
        window // 8,
        blend,
        (tuple([zero + 1.0] * parts_n), tuple([zero] * (3 * parts_n))),
    )
    pred = [
        jnp.concatenate([image[ch * parts_n + part] for part in range(parts_n)], axis=0)
        for ch in range(3)
    ]
    for ch in range(3):
        halo_out[0, ch] = pred[ch][0:REACH]
        halo_out[1, ch] = pred[ch][rows - REACH : rows]
    edges_start(halo_out, halo_in, 1)
    edges_wait(thalo_out, thalo_in, 0)
    edges_wait(halo_out, halo_in, 1)

    in_rows, mid_rows = up8(rows + 2 * REACH), up8(rows + REACH)
    fill = jnp.zeros((in_rows - rows - 2 * REACH, cols), F32)
    mine = target_ref[0]
    ext_x = jnp.concatenate(
        [v for ch in range(3) for v in (halo_in[0, ch], pred[ch], halo_in[1, ch], fill)], axis=0
    )
    ext_y = jnp.concatenate(
        [v for ch in range(3) for v in (thalo_in[0, ch], mine[ch], thalo_in[1, ch], fill)], axis=0
    )
    fields = jnp.concatenate(
        [ext_x, ext_y, ext_x * ext_x, ext_y * ext_y, ext_x * ext_y], axis=1
    )
    down = jnp.dot(first_ref[...], fields, precision=HIGHEST_MODE, preferred_element_type=F32)
    stacked = jnp.concatenate([down[:, f * cols : (f + 1) * cols] for f in range(5)], axis=0)
    smoothed = jnp.dot(
        stacked, across_ref[...], precision=HIGHEST_MODE, preferred_element_type=F32
    )
    high = 3 * mid_rows
    mean_x, mean_y, square_x, square_y, cross = [
        smoothed[f * high : (f + 1) * high] for f in range(5)
    ]
    n_mean = 2.0 * mean_x * mean_y + STAB_MEAN
    n_var = 2.0 * (cross - mean_x * mean_y) + STAB_VAR
    d_mean = mean_x * mean_x + mean_y * mean_y + STAB_MEAN
    d_var = (square_x - mean_x * mean_x) + (square_y - mean_y * mean_y) + STAB_VAR
    inv_mean = 1.0 / d_mean
    inv_var = 1.0 / d_var
    inverse = inv_mean * inv_var
    ssim = n_mean * n_var * inverse
    ext_row = lax.broadcasted_iota(jnp.int32, (high, cols), 0) % mid_rows
    image_row = ext_row + (band * rows - HALO)
    inside = (image_row >= 0) & (image_row < bands_n * rows) & (ext_row < rows + REACH)
    scale = -SSIM_WEIGHT / 3.0
    part_mean = 2.0 * mean_y * (n_var - n_mean) * inverse - 2.0 * mean_x * ssim * (
        inv_mean - inv_var
    )
    adjoint = jnp.concatenate(
        [
            jnp.where(inside, scale * part_mean, 0.0),
            jnp.where(inside, -scale * ssim * inv_var, 0.0),
            jnp.where(inside, (2.0 * scale) * n_mean * inverse, 0.0),
        ],
        axis=1,
    )
    down2 = jnp.dot(second_ref[...], adjoint, precision=HIGHEST_MODE, preferred_element_type=F32)
    stacked2 = jnp.concatenate([down2[:, f * cols : (f + 1) * cols] for f in range(3)], axis=0)
    spread = jnp.dot(
        stacked2, across_ref[...], precision=HIGHEST_MODE, preferred_element_type=F32
    )
    deep = 3 * rows
    pred_all = jnp.concatenate(pred, axis=0)
    mine_all = jnp.concatenate([mine[ch] for ch in range(3)], axis=0)
    error = pred_all - mine_all
    sign = jnp.where(error > 0.0, 1.0, jnp.where(error < 0.0, -1.0, 0.0))
    grad_pred = (
        ABS_WEIGHT / 3.0 * sign
        + spread[0:deep]
        + 2.0 * pred_all * spread[deep : 2 * deep]
        + mine_all * spread[2 * deep : 3 * deep]
    )
    own = (ext_row >= HALO) & (ext_row < HALO + rows)
    loss = jnp.sum(ABS_WEIGHT / 3.0 * jnp.abs(error), keepdims=True) + jnp.sum(
        jnp.where(own, SSIM_WEIGHT / 3.0 * (1.0 - ssim), 0.0), keepdims=True
    )

    pull = [
        [grad_pred[ch * rows + 8 * part : ch * rows + 8 * part + 8] for part in range(parts_n)]
        for ch in range(3)
    ]

    def unblend(step, behind):
        group = window // 8 - 1 - step
        behind = list(behind)
        sums = [[None] * 8 for _ in range(6)]
        for k in reversed(range(8)):
            j = group * 8 + k
            tint = [spread_row(3 + ch, j) for ch in range(3)]
            totals = [None] * 6
            for part in range(parts_n):
                alpha = alpha_s[j, part]
                trans = trans_s[j, part]
                shade = (
                    tint[0] * pull[0][part] + tint[1] * pull[1][part] + tint[2] * pull[2][part]
                )
                gap = shade - behind[part]
                behind[part] = behind[part] + alpha * gap
                weight = alpha * trans
                lean = weight * gap
                lean_r = lean * row_local[part]
                terms = [lean, lean_r, lean_r * row_local[part]]
                terms += [weight * pull[ch][part] for ch in range(3)]
                totals = [
                    term if total is None else total + term for term, total in zip(terms, totals)
                ]
            for kind in range(6):
                sums[kind][k] = totals[kind]
        at = pl.multiple_of(group * 8, 8)
        for kind in range(6):
            moment_s[kind, pl.ds(at, 8), :] = tree_sum(sums[kind], cols)
        return tuple(behind)

    lax.fori_loop(0, window // 8, unblend, tuple([zero] * parts_n))

    by_x = exact_dot(power, moment_s[0], NT)
    m_00, m_10, m_20 = by_x[0:tiles], by_x[tiles : 2 * tiles], by_x[2 * tiles : 3 * tiles]
    by_xr = exact_dot(power[0 : 2 * tiles], moment_s[1], NT)
    m_01, m_11 = by_xr[0:tiles], by_xr[tiles : 2 * tiles]
    m_02 = exact_dot(power[0:tiles], moment_s[2], NT)
    s_x = m_10 - u_rel * m_00
    s_y = m_01 - w_rel * m_00
    s_xx = m_20 - 2.0 * u_rel * m_10 + u_rel * u_rel * m_00
    s_xy = m_11 - u_rel * m_01 - w_rel * m_10 + u_rel * w_rel * m_00
    s_yy = m_02 - 2.0 * w_rel * m_01 + w_rel * w_rel * m_00
    by_det = -(coef_a * s_xx + coef_b * s_xy + coef_c * s_yy) * inv_det
    derivs = [
        -(2.0 * coef_a * s_x + coef_b * s_y),
        -(2.0 * coef_c * s_y + coef_b * s_x),
        -0.5 * inv_det * s_yy + by_det * c_c,
        inv_det * s_xy - 2.0 * c_b * by_det,
        -0.5 * inv_det * s_xx + by_det * c_a,
        m_00 / opac,
    ] + [exact_dot(power[0:tiles], moment_s[3 + ch], NT) for ch in range(3)]
    for p in range(ROW_REC):
        split_pairs = jnp.concatenate(
            [derivs[p][:, k * block_len : (k + 1) * block_len] for k in range(TILE_MOST)], axis=0
        )
        routed = exact_dot(put_owner, split_pairs, NN)
        for h in range(halves):
            grad_out[:, p * halves + h, :] = routed[:, h * 128 : (h + 1) * 128]
    grad_out[:, ROW_REC * halves, :] = jnp.broadcast_to(loss, (devices, 128))
    to_all(lambda peer: grad_out.at[peer], grad_in, 2)
    grad_in[me] = grad_out[me]
    wait_all(grad_in, 2)
    incoming_ref[...] = grad_in[...]


def adam_kernel(
    geometry,
    messages_ref,
    incoming_ref,
    rates_ref,
    gauss_ref,
    one_ref,
    two_ref,
    out_gauss,
    out_one,
    out_two,
    out_loss,
    out_grad,
):
    views_n, bands_n, blocks, list_len, rows, cols, block_len = geometry
    devices = views_n * bands_n
    halves = block_len // 128
    me = lax.axis_index("view") * bands_n + lax.axis_index("band")
    base = (me * blocks).astype(F32)
    asked = messages_ref[...]
    hot = requests_of(asked, base, list_len, blocks)
    missing = 1.0 - jnp.max(hot, axis=1, keepdims=True)
    cam = [asked[:, c : c + 1] for c in range(9)]

    def picked(component):
        return exact_dot(hot, gauss_ref[:, component, :], NN)

    def arrived(p):
        return jnp.concatenate(
            [incoming_ref[:, p * halves + h, :] for h in range(halves)], axis=1
        )

    d_u, d_w = arrived(0), arrived(1)
    columns = []
    along = [cam[c] * d_u + cam[3 + c] * d_w for c in range(3)]
    columns += along + [cam[8] * value for value in along]
    quats = [picked(9 + c) for c in range(4)]
    quats[0] = quats[0] + missing
    logs = [picked(6 + c) for c in range(3)]
    _, pullback = jax.vjp(
        lambda a, b, c: shape_of(cam[0:6], a, b, c), logs, quats, picked(13)
    )
    d_logs, d_quats, d_logit = pullback(tuple(arrived(2 + p) for p in range(4)))
    columns += list(d_logs) + list(d_quats) + [d_logit]
    turned = jnp.transpose(jnp.concatenate([asked] * 3, axis=0))
    hot_t = jnp.transpose(hot)
    for c in range(14):
        out_grad[:, c, :] = exact_dot(hot_t, columns[c], NN)
    basis = camera_basis([turned[c : c + 1, :] for c in range(6)])
    channel = lax.broadcasted_iota(jnp.int32, (3, 3 * devices), 1) // devices
    own_channel = channel == lax.broadcasted_iota(jnp.int32, (3, 3 * devices), 0)
    fan = jnp.concatenate([jnp.where(own_channel, value, 0.0) for value in basis], axis=0)
    hot_3 = jnp.transpose(jnp.concatenate([hot] * 3, axis=0))
    routed = jnp.concatenate([hot_3[b : b + 1, :] * fan for b in range(blocks)], axis=0)
    tinted = jnp.concatenate([arrived(6 + ch) for ch in range(3)], axis=0)
    colour = jnp.dot(routed, tinted, precision=HIGHEST_MODE, preferred_element_type=F32)
    shades = fan.shape[0]
    for b in range(blocks):
        out_grad[b, 14:, :] = colour[b * shades : (b + 1) * shades]
    losses = incoming_ref[:, ROW_REC * halves, :]
    out_loss[...] = jnp.sum(losses, axis=0, keepdims=True)[:, 0:1] * (
        1.0 / (devices * rows * cols)
    )
    rates = rates_ref[...]

    def update(b, carry):
        gradient = out_grad[b]
        new_one = 0.9 * one_ref[b] + 0.1 * gradient
        new_two = 0.999 * two_ref[b] + 0.001 * gradient * gradient
        out_one[b] = new_one
        out_two[b] = new_two
        change = rates * (new_one / BIAS_FIRST) / (jnp.sqrt(new_two / BIAS_SECOND) + 1e-08)
        out_gauss[b] = gauss_ref[b] - change
        return carry

    lax.fori_loop(0, blocks, update, 0)


def per_device(
    gaussians,
    first_moment,
    second_moment,
    camera,
    target,
    block_list,
    block_count,
    tile_start,
    tile_end,
):
    views_n = lax.axis_size("view")
    bands_n = lax.axis_size("band")
    devices = views_n * bands_n
    blocks, comps, block_len = gaussians.shape
    list_len = block_list.shape[2]
    rows, cols = target.shape[2:]
    tiles = cols // TILE
    pairs = TILE_MOST * tiles
    halves = block_len // 128
    geometry = (views_n, bands_n, blocks, list_len, rows, cols, block_len)

    message = jnp.concatenate(
        [
            camera,
            jnp.zeros((1, 7), F32),
            block_list[0].astype(F32),
            jnp.zeros((1, 128 - 16 - list_len), F32),
        ],
        axis=1,
    )
    spot = tile_start[0, 0][None, :] + jnp.arange(TILE_MOST, dtype=jnp.int32)[:, None]
    spot = jnp.where(spot < tile_end[0, 0][None, :], spot, -1).reshape(pairs, 1)
    place = (spot == jnp.arange(128, dtype=jnp.int32)[None, :]).astype(F32)
    table = jnp.concatenate([message, place], axis=0)[:, None, :]

    across, first, second = smoothing_tables(rows, cols, 3)
    power = power_table(tiles, cols)
    vmem = pl.BlockSpec(memory_space=pltpu.VMEM)
    rec_rows = ROW_REC * halves
    window = TILE_MOST * block_len
    incoming, messages = pl.pallas_call(
        functools.partial(step_kernel, geometry),
        out_shape=(
            jax.ShapeDtypeStruct((devices, rec_rows + 1, 128), F32),
            jax.ShapeDtypeStruct((devices, 128), F32),
        ),
        in_specs=[vmem] * 7,
        out_specs=(vmem, vmem),
        scratch_shapes=[
            pltpu.VMEM((devices, 1, 128), F32),
            pltpu.VMEM((devices, rec_rows, 128), F32),
            pltpu.VMEM((devices, rec_rows, 128), F32),
            pltpu.VMEM((devices, rec_rows + 1, 128), F32),
            pltpu.VMEM((devices, rec_rows + 1, 128), F32),
            pltpu.VMEM((2, 3, REACH, cols), F32),
            pltpu.VMEM((2, 3, REACH, cols), F32),
            pltpu.VMEM((2, 3, REACH, cols), F32),
            pltpu.VMEM((2, 3, REACH, cols), F32),
            pltpu.VMEM((6, window, cols), F32),
            pltpu.VMEM((window, rows // 8, 8, cols), F32),
            pltpu.VMEM((window, rows // 8, 8, cols), F32),
            pltpu.VMEM((6, window, cols), F32),
            pltpu.SemaphoreType.DMA((3,)),
            pltpu.SemaphoreType.DMA((3,)),
            pltpu.SemaphoreType.DMA((2, 2)),
            pltpu.SemaphoreType.DMA((2, 2)),
        ],
        compiler_params=pltpu.CompilerParams(collective_id=0, has_side_effects=True),
        name="render_step",
    )(table, target, gaussians, across, first, second, power)

    rates = np.ascontiguousarray(np.broadcast_to(learning_rates()[:, None], (comps, block_len)))
    shape = jax.ShapeDtypeStruct(gaussians.shape, F32)
    new_params, new_one, new_two, mean_loss, gradient = pl.pallas_call(
        functools.partial(adam_kernel, geometry),
        out_shape=(shape, shape, shape, jax.ShapeDtypeStruct((1, 1), F32), shape),
        in_specs=[vmem] * 6,
        out_specs=(vmem,) * 5,
        name="adam_step",
    )(messages, incoming, rates, gaussians, first_moment, second_moment)
    return (new_params, new_one, new_two, mean_loss.reshape(()), gradient)


def solution(mesh):
    return jax.shard_map(
        per_device,
        mesh=mesh,
        in_specs=(
            P(("view", "band"), None, None),
            P(("view", "band"), None, None),
            P(("view", "band"), None, None),
            P("view", None),
            P("view", None, "band", None),
            P("view", "band", None),
            P("view", "band"),
            P("view", "band", None),
            P("view", "band", None),
        ),
        out_specs=(
            P(("view", "band"), None, None),
            P(("view", "band"), None, None),
            P(("view", "band"), None, None),
            P(),
            P(("view", "band"), None, None),
        ),
        check_vma=False,
    )
```

```python
import functools
import math

import jax
import jax.numpy as jnp
import numpy as np
from jax import lax
from jax.experimental import pallas as pl
from jax.experimental.pallas import tpu as pltpu
from jax.sharding import PartitionSpec as P

TILE = 16
TILE_MOST = 2
HALO = 5
REACH = 2 * HALO
ROW_REC = 9
PIECES = 4

HIGHEST_MODE = lax.Precision.HIGHEST
SSIM_WEIGHT = 0.2
ABS_WEIGHT = 0.8
STAB_MEAN = 0.0001
STAB_VAR = 0.0009
BIAS_FIRST = 1.0 - math.exp(100.0 * math.log(0.9))
BIAS_SECOND = 1.0 - math.exp(100.0 * math.log(0.999))
LOG2_E = math.log2(math.e)
SH_ZERO = 0.28209479177387814
SH_ONE = 0.4886025119029199
SH_TWO = [
    1.0925484305920792,
    -1.0925484305920792,
    0.31539156525252005,
    -1.0925484305920792,
    0.5462742152960396,
]
SH_THREE = [
    -0.5900435899266435,
    2.890611442640554,
    -0.4570457994644658,
    0.3731763325901154,
    -0.4570457994644658,
    1.445305721320277,
    -0.5900435899266435,
]
F32 = jnp.float32
BF16 = jnp.bfloat16
MESH = pl.DeviceIdType.MESH
NEVER = -1e30


def learning_rates():
    return np.concatenate(
        [
            np.full(6, 0.016),
            np.full(3, 0.005),
            np.full(4, 0.001),
            np.full(1, 0.05),
            np.full(3, 0.0025),
            np.full(45, 0.000125),
        ]
    ).astype(np.float32)


def kernel_taps():
    raw_taps = [math.exp(-(offset * offset) / 4.5) for offset in range(-5, 6)]
    tap_total = sum(raw_taps)
    return [raw_tap / tap_total for raw_tap in raw_taps]


def up8(value):
    return (value + 7) // 8 * 8


def smoothing_tables(rows, cols, channels):
    taps = kernel_taps()
    in_rows, mid_rows = up8(rows + 2 * REACH), up8(rows + REACH)
    across = np.zeros((cols, cols), np.float32)
    for out in range(cols):
        for m in range(-HALO, HALO + 1):
            if 0 <= out + m < cols:
                across[out + m, out] = taps[m + HALO]
    first = np.zeros((channels * mid_rows, channels * in_rows), np.float32)
    second = np.zeros((channels * rows, channels * mid_rows), np.float32)
    for c in range(channels):
        for e in range(rows + REACH):
            for m in range(REACH + 1):
                first[c * mid_rows + e, c * in_rows + e + m] = taps[m]
        for i in range(rows):
            for m in range(REACH + 1):
                second[c * rows + i, c * mid_rows + i + m] = taps[m]
    return across, first, second


def power_table(tiles, cols):
    lane = np.arange(cols)
    local = lane % TILE + 0.5 - TILE / 2
    belongs = (lane[None, :] // TILE == np.arange(tiles)[:, None]).astype(np.float32)
    return np.concatenate([belongs, belongs * local, belongs * local * local]).astype(np.float32)


def harmonics(dir_x, dir_y, dir_z):
    sq_x, sq_y, sq_z = (dir_x * dir_x, dir_y * dir_y, dir_z * dir_z)
    return [
        SH_ZERO + 0.0 * dir_x,
        -SH_ONE * dir_y,
        SH_ONE * dir_z,
        -SH_ONE * dir_x,
        SH_TWO[0] * dir_x * dir_y,
        SH_TWO[1] * dir_y * dir_z,
        SH_TWO[2] * (2.0 * sq_z - sq_x - sq_y),
        SH_TWO[3] * dir_x * dir_z,
        SH_TWO[4] * (sq_x - sq_y),
        SH_THREE[0] * dir_y * (3.0 * sq_x - sq_y),
        SH_THREE[1] * dir_x * dir_y * dir_z,
        SH_THREE[2] * dir_y * (4.0 * sq_z - sq_x - sq_y),
        SH_THREE[3] * dir_z * (2.0 * sq_z - 3.0 * sq_x - 3.0 * sq_y),
        SH_THREE[4] * dir_x * (4.0 * sq_z - sq_x - sq_y),
        SH_THREE[5] * dir_z * (sq_x - sq_y),
        SH_THREE[6] * dir_x * (sq_x - 3.0 * sq_y),
    ]


def camera_basis(affine):
    a, b = affine[0:3], affine[3:6]
    n_x = a[1] * b[2] - a[2] * b[1]
    n_y = a[2] * b[0] - a[0] * b[2]
    n_z = a[0] * b[1] - a[1] * b[0]
    length = jnp.sqrt(n_x * n_x + n_y * n_y + n_z * n_z)
    return harmonics(n_x / length, n_y / length, n_z / length)


def shape_of(affine, logs, quats, logit):
    scales = [jnp.exp(value) for value in logs]
    quat_len = jnp.sqrt(
        quats[0] * quats[0] + quats[1] * quats[1] + quats[2] * quats[2] + quats[3] * quats[3]
    )
    r, i, j, k = [value / quat_len for value in quats]
    rotation = [
        [1.0 - 2.0 * (j * j + k * k), 2.0 * (i * j - r * k), 2.0 * (i * k + r * j)],
        [2.0 * (i * j + r * k), 1.0 - 2.0 * (i * i + k * k), 2.0 * (j * k - r * i)],
        [2.0 * (i * k - r * j), 2.0 * (j * k + r * i), 1.0 - 2.0 * (i * i + j * j)],
    ]
    m = [
        [
            (
                affine[3 * o] * rotation[0][c]
                + affine[3 * o + 1] * rotation[1][c]
                + affine[3 * o + 2] * rotation[2][c]
            )
            * scales[c]
            for c in range(3)
        ]
        for o in range(2)
    ]
    conic_a = m[0][0] * m[0][0] + m[0][1] * m[0][1] + m[0][2] * m[0][2] + 0.3
    conic_b = m[0][0] * m[1][0] + m[0][1] * m[1][1] + m[0][2] * m[1][2]
    conic_c = m[1][0] * m[1][0] + m[1][1] * m[1][1] + m[1][2] * m[1][2] + 0.3
    opacity = 1.0 / (1.0 + jnp.exp(-logit))
    return conic_a, conic_b, conic_c, opacity


def split3(value, axis=0):
    high = value.astype(BF16)
    rest = value - high.astype(F32)
    middle = rest.astype(BF16)
    low = (rest - middle.astype(F32)).astype(BF16)
    return high, middle, low


def exact_dot(table, value, dims):
    table = table.astype(BF16)
    total = None
    for part in split3(value):
        term = lax.dot_general(table, part, (dims, ((), ())), preferred_element_type=F32)
        total = term if total is None else total + term
    return total


def expand_dot(value, table):
    table = table.astype(BF16)
    total = None
    for part in split3(value):
        term = lax.dot_general(
            part, table, (((0,), (0,)), ((), ())), preferred_element_type=F32
        )
        total = term if total is None else total + term
    return total


NN = ((1,), (0,))
NT = ((1,), (1,))


def requests_of(messages, base, list_len, blocks):
    devices = messages.shape[0]
    block_iota = lax.broadcasted_iota(jnp.int32, (devices, blocks), 1).astype(F32) + base
    hit = jnp.zeros((devices, blocks), F32)
    for i in range(list_len):
        wanted = messages[:, 16 + i : 17 + i]
        hit = hit + jnp.where(wanted == block_iota, 1.0, 0.0)
    return hit


def tree_sum(vregs, lane_count):
    sub = lax.broadcasted_iota(jnp.int32, (8, lane_count), 0)

    def join(a, b, mask, shift):
        return jnp.where(mask, a, b) + pltpu.roll(jnp.where(mask, b, a), 8 - shift, 0)

    def half(offset):
        return ((sub + (8 - offset)) % 8) < 4

    def quarter(offset):
        return ((sub + (8 - offset)) % 4) < 2

    z1 = join(
        join(vregs[0], vregs[4], half(0), 4), join(vregs[2], vregs[6], half(2), 4), quarter(0), 2
    )
    z2 = join(
        join(vregs[1], vregs[5], half(1), 4), join(vregs[3], vregs[7], half(3), 4), quarter(1), 2
    )
    return join(z1, z2, (sub % 2) < 1, 1)


def step_kernel(
    geometry,
    table_ref,
    target_ref,
    gauss_ref,
    across_ref,
    first_ref,
    second_ref,
    power_ref,
    incoming_ref,
    messages_ref,
    msg_in,
    rec_out,
    rec_in,
    grad_out,
    grad_in,
    halo_out,
    halo_in,
    thalo_out,
    thalo_in,
    coef,
    alpha_s,
    trans_s,
    moment_s,
    send_sem,
    recv_sem,
    halo_send,
    halo_recv,
):
    views_n, bands_n, blocks, list_len, rows, cols, block_len = geometry
    devices = views_n * bands_n
    tiles = cols // TILE
    pairs = TILE_MOST * tiles
    window = TILE_MOST * block_len
    halves = block_len // 128
    view = lax.axis_index("view")
    band = lax.axis_index("band")
    me = view * bands_n + band
    base = (me * blocks).astype(F32)
    has_up = band > 0
    has_down = band < bands_n - 1

    def peer_of(d):
        peer = lax.rem(me + d, devices)
        return (peer // bands_n, lax.rem(peer, bands_n))

    halo_in[...] = jnp.zeros_like(halo_in)
    thalo_in[...] = jnp.zeros_like(thalo_in)
    thalo_out[0] = target_ref[0, :, 0:REACH, :]
    thalo_out[1] = target_ref[0, :, rows - REACH : rows, :]
    barrier = pltpu.get_barrier_semaphore()

    def greet(d, carry):
        pl.semaphore_signal(barrier, inc=1, device_id=peer_of(d), device_id_type=MESH)
        return carry

    lax.fori_loop(1, devices, greet, 0)
    pl.semaphore_wait(barrier, devices - 1)

    def to_all(source_of, landing, phase):
        def send(d, carry):
            peer = lax.rem(me + d, devices)
            pltpu.make_async_remote_copy(
                src_ref=source_of(peer),
                dst_ref=landing.at[me],
                send_sem=send_sem.at[phase],
                recv_sem=recv_sem.at[phase],
                device_id=peer_of(d),
                device_id_type=MESH,
            ).start()
            return carry

        lax.fori_loop(1, devices, send, 0)

    def wait_all(landing, phase):
        every = landing.at[pl.ds(0, devices - 1)]
        pltpu.make_async_copy(every, every, recv_sem.at[phase]).wait()
        pltpu.make_async_copy(every, every, send_sem.at[phase]).wait()

    def edge_copy(source, landing, direction, phase):
        step = -1 if direction == 0 else 1
        return pltpu.make_async_remote_copy(
            src_ref=source.at[direction],
            dst_ref=landing.at[1 - direction],
            send_sem=halo_send.at[phase, direction],
            recv_sem=halo_recv.at[phase, 1 - direction],
            device_id=(view, band + step),
            device_id_type=MESH,
        )

    def edges_start(source, landing, phase):
        @pl.when(has_up)
        def _():
            edge_copy(source, landing, 0, phase).start()

        @pl.when(has_down)
        def _():
            edge_copy(source, landing, 1, phase).start()

    def edges_wait(source, landing, phase):
        @pl.when(has_up)
        def _():
            up = edge_copy(source, landing, 0, phase)
            up.wait_send()
            pltpu.make_async_copy(
                landing.at[0], landing.at[0], halo_recv.at[phase, 0]
            ).wait()

        @pl.when(has_down)
        def _():
            down = edge_copy(source, landing, 1, phase)
            down.wait_send()
            pltpu.make_async_copy(
                landing.at[1], landing.at[1], halo_recv.at[phase, 1]
            ).wait()

    message = table_ref.at[0]
    to_all(lambda peer: message, msg_in, 0)
    edges_start(thalo_out, thalo_in, 0)
    msg_in[me] = table_ref[0]

    list_row = table_ref[0][:, 16 : 16 + list_len]
    owner_low = lax.broadcasted_iota(jnp.int32, (devices, list_len), 0).astype(F32) * blocks
    owner_hot = jnp.where((list_row >= owner_low) & (list_row < owner_low + blocks), 1.0, 0.0)
    place = jnp.concatenate(
        [table_ref[1 + pair][:, 0:list_len] for pair in range(pairs)], axis=0
    )
    live_pair = jnp.max(place, axis=1, keepdims=True)
    pick_owner = lax.dot_general(
        place.astype(BF16), owner_hot.astype(BF16), (NT, ((), ())), preferred_element_type=F32
    )
    put_owner = lax.dot_general(
        owner_hot.astype(BF16), place.astype(BF16), (NT, ((), ())), preferred_element_type=F32
    )
    live = jnp.concatenate(
        [
            jnp.broadcast_to(live_pair[k * tiles : (k + 1) * tiles], (tiles, block_len))
            for k in range(TILE_MOST)
        ],
        axis=1,
    )

    wait_all(msg_in, 0)

    asked = msg_in[...].reshape(devices, 128)
    messages_ref[...] = asked
    hot = requests_of(asked, base, list_len, blocks)
    missing = 1.0 - jnp.max(hot, axis=1, keepdims=True)
    cam = [asked[:, c : c + 1] for c in range(9)]

    def picked(component):
        return exact_dot(hot, gauss_ref[component], NN)

    centre = [picked(c) + cam[8] * picked(3 + c) for c in range(3)]
    records = [
        cam[0] * centre[0] + cam[1] * centre[1] + cam[2] * centre[2] + cam[6],
        cam[3] * centre[0] + cam[4] * centre[1] + cam[5] * centre[2] + cam[7],
    ]
    quats = [picked(9 + c) for c in range(4)]
    quats[0] = quats[0] + missing
    conic_a, conic_b, conic_c, opacity = shape_of(
        cam[0:6], [picked(6 + c) for c in range(3)], quats, picked(13)
    )
    records += [conic_a, conic_b, conic_c, opacity]
    basis = camera_basis(cam)
    basis = [jnp.where(missing > 0.5, 0.0, value) for value in basis]
    for ch in range(3):
        colour = 0.5
        for q in range(16):
            colour = colour + basis[q] * picked(14 + 3 * q + ch)
        records.append(colour)
    for p in range(ROW_REC):
        for h in range(halves):
            rec_out[:, p * halves + h, :] = records[p][:, h * 128 : (h + 1) * 128]
    to_all(lambda peer: rec_out.at[peer], rec_in, 1)
    rec_in[me] = rec_out[me]
    wait_all(rec_in, 1)

    def gathered(p):
        parts = []
        for h in range(halves):
            parts.append(exact_dot(pick_owner, rec_in[:, p * halves + h, :], NN))
        whole = jnp.concatenate(parts, axis=1)
        return jnp.concatenate(
            [whole[k * tiles : (k + 1) * tiles] for k in range(TILE_MOST)], axis=1
        )

    dead = 1.0 - live
    tile_row = lax.broadcasted_iota(jnp.int32, (tiles, window), 0).astype(F32)
    u_rel = gathered(0) - (tile_row * TILE + 0.5 * TILE)
    w_rel = gathered(1) - ((band * rows).astype(F32) + 0.5 * TILE)
    c_a = gathered(2) + dead
    c_b = gathered(3)
    c_c = gathered(4) + dead
    opac = gathered(5) + dead
    inv_det = 1.0 / (c_a * c_c - c_b * c_b)
    coef_a = -0.5 * c_c * inv_det
    coef_b = c_b * inv_det
    coef_c = -0.5 * c_a * inv_det
    keep = live > 0.5

    def masked(value, other=0.0):
        return jnp.where(keep, value, other)

    flat = LOG2_E * (
        coef_a * u_rel * u_rel + coef_b * u_rel * w_rel + coef_c * w_rel * w_rel
    ) + LOG2_E * jnp.log(opac)
    power = power_ref[...]
    coef[0] = expand_dot(
        jnp.concatenate(
            [
                masked(flat, NEVER),
                masked(LOG2_E * (-2.0 * coef_a * u_rel - coef_b * w_rel)),
                masked(LOG2_E * coef_a),
            ],
            axis=0,
        ),
        power,
    )
    coef[1] = expand_dot(
        jnp.concatenate(
            [
                masked(LOG2_E * (-coef_b * u_rel - 2.0 * coef_c * w_rel)),
                masked(LOG2_E * coef_b),
            ],
            axis=0,
        ),
        power[0 : 2 * tiles],
    )
    coef[2] = expand_dot(masked(LOG2_E * coef_c), power[0:tiles])
    for ch in range(3):
        coef[3 + ch] = expand_dot(masked(gathered(6 + ch)), power[0:tiles])

    sub8 = lax.broadcasted_iota(jnp.int32, (8, cols), 0).astype(F32)
    parts_n = rows // 8
    row_local = [sub8 + (8.0 * part + 0.5 - 0.5 * TILE) for part in range(parts_n)]

    def spread_row(kind, j):
        return coef[kind, pl.ds(j, 8, stride=0), :]

    def blend(group, carry):
        trans, image = carry
        trans, image = list(trans), list(image)
        for k in range(8):
            j = group * 8 + k
            q0, q1, q2 = spread_row(0, j), spread_row(1, j), spread_row(2, j)
            tint = [spread_row(3 + ch, j) for ch in range(3)]
            for part in range(parts_n):
                r = row_local[part]
                alpha = jnp.exp2(q0 + r * (q1 + r * q2))
                weight = alpha * trans[part]
                alpha_s[j, part] = alpha
                trans_s[j, part] = trans[part]
                trans[part] = trans[part] - weight
                for ch in range(3):
                    at = ch * parts_n + part
                    image[at] = image[at] + weight * tint[ch]
        return tuple(trans), tuple(image)

    zero = jnp.zeros((8, cols), F32)
    _, image = lax.fori_loop(
        0,
        window // 8,
        blend,
        (tuple([zero + 1.0] * parts_n), tuple([zero] * (3 * parts_n))),
    )
    pred = [
        jnp.concatenate([image[ch * parts_n + part] for part in range(parts_n)], axis=0)
        for ch in range(3)
    ]
    for ch in range(3):
        halo_out[0, ch] = pred[ch][0:REACH]
        halo_out[1, ch] = pred[ch][rows - REACH : rows]
    edges_start(halo_out, halo_in, 1)
    edges_wait(thalo_out, thalo_in, 0)
    edges_wait(halo_out, halo_in, 1)

    in_rows, mid_rows = up8(rows + 2 * REACH), up8(rows + REACH)
    fill = jnp.zeros((in_rows - rows - 2 * REACH, cols), F32)
    mine = target_ref[0]
    ext_x = jnp.concatenate(
        [v for ch in range(3) for v in (halo_in[0, ch], pred[ch], halo_in[1, ch], fill)], axis=0
    )
    ext_y = jnp.concatenate(
        [v for ch in range(3) for v in (thalo_in[0, ch], mine[ch], thalo_in[1, ch], fill)], axis=0
    )
    fields = jnp.concatenate(
        [ext_x, ext_y, ext_x * ext_x, ext_y * ext_y, ext_x * ext_y], axis=1
    )
    down = jnp.dot(first_ref[...], fields, precision=HIGHEST_MODE, preferred_element_type=F32)
    stacked = jnp.concatenate([down[:, f * cols : (f + 1) * cols] for f in range(5)], axis=0)
    smoothed = jnp.dot(
        stacked, across_ref[...], precision=HIGHEST_MODE, preferred_element_type=F32
    )
    high = 3 * mid_rows
    mean_x, mean_y, square_x, square_y, cross = [
        smoothed[f * high : (f + 1) * high] for f in range(5)
    ]
    n_mean = 2.0 * mean_x * mean_y + STAB_MEAN
    n_var = 2.0 * (cross - mean_x * mean_y) + STAB_VAR
    d_mean = mean_x * mean_x + mean_y * mean_y + STAB_MEAN
    d_var = (square_x - mean_x * mean_x) + (square_y - mean_y * mean_y) + STAB_VAR
    inv_mean = 1.0 / d_mean
    inv_var = 1.0 / d_var
    inverse = inv_mean * inv_var
    ssim = n_mean * n_var * inverse
    ext_row = lax.broadcasted_iota(jnp.int32, (high, cols), 0) % mid_rows
    image_row = ext_row + (band * rows - HALO)
    inside = (image_row >= 0) & (image_row < bands_n * rows) & (ext_row < rows + REACH)
    scale = -SSIM_WEIGHT / 3.0
    part_mean = 2.0 * mean_y * (n_var - n_mean) * inverse - 2.0 * mean_x * ssim * (
        inv_mean - inv_var
    )
    adjoint = jnp.concatenate(
        [
            jnp.where(inside, scale * part_mean, 0.0),
            jnp.where(inside, -scale * ssim * inv_var, 0.0),
            jnp.where(inside, (2.0 * scale) * n_mean * inverse, 0.0),
        ],
        axis=1,
    )
    down2 = jnp.dot(second_ref[...], adjoint, precision=HIGHEST_MODE, preferred_element_type=F32)
    stacked2 = jnp.concatenate([down2[:, f * cols : (f + 1) * cols] for f in range(3)], axis=0)
    spread = jnp.dot(
        stacked2, across_ref[...], precision=HIGHEST_MODE, preferred_element_type=F32
    )
    deep = 3 * rows
    pred_all = jnp.concatenate(pred, axis=0)
    mine_all = jnp.concatenate([mine[ch] for ch in range(3)], axis=0)
    error = pred_all - mine_all
    sign = jnp.where(error > 0.0, 1.0, jnp.where(error < 0.0, -1.0, 0.0))
    grad_pred = (
        ABS_WEIGHT / 3.0 * sign
        + spread[0:deep]
        + 2.0 * pred_all * spread[deep : 2 * deep]
        + mine_all * spread[2 * deep : 3 * deep]
    )
    own = (ext_row >= HALO) & (ext_row < HALO + rows)
    loss = jnp.sum(ABS_WEIGHT / 3.0 * jnp.abs(error), keepdims=True) + jnp.sum(
        jnp.where(own, SSIM_WEIGHT / 3.0 * (1.0 - ssim), 0.0), keepdims=True
    )

    pull = [
        [grad_pred[ch * rows + 8 * part : ch * rows + 8 * part + 8] for part in range(parts_n)]
        for ch in range(3)
    ]

    def unblend(step, behind):
        group = window // 8 - 1 - step
        behind = list(behind)
        sums = [[None] * 8 for _ in range(6)]
        for k in reversed(range(8)):
            j = group * 8 + k
            tint = [spread_row(3 + ch, j) for ch in range(3)]
            totals = [None] * 6
            for part in range(parts_n):
                alpha = alpha_s[j, part]
                trans = trans_s[j, part]
                shade = (
                    tint[0] * pull[0][part] + tint[1] * pull[1][part] + tint[2] * pull[2][part]
                )
                gap = shade - behind[part]
                behind[part] = behind[part] + alpha * gap
                weight = alpha * trans
                lean = weight * gap
                lean_r = lean * row_local[part]
                terms = [lean, lean_r, lean_r * row_local[part]]
                terms += [weight * pull[ch][part] for ch in range(3)]
                totals = [
                    term if total is None else total + term for term, total in zip(terms, totals)
                ]
            for kind in range(6):
                sums[kind][k] = totals[kind]
        at = pl.multiple_of(group * 8, 8)
        for kind in range(6):
            moment_s[kind, pl.ds(at, 8), :] = tree_sum(sums[kind], cols)
        return tuple(behind)

    lax.fori_loop(0, window // 8, unblend, tuple([zero] * parts_n))

    by_x = exact_dot(power, moment_s[0], NT)
    m_00, m_10, m_20 = by_x[0:tiles], by_x[tiles : 2 * tiles], by_x[2 * tiles : 3 * tiles]
    by_xr = exact_dot(power[0 : 2 * tiles], moment_s[1], NT)
    m_01, m_11 = by_xr[0:tiles], by_xr[tiles : 2 * tiles]
    m_02 = exact_dot(power[0:tiles], moment_s[2], NT)
    s_x = m_10 - u_rel * m_00
    s_y = m_01 - w_rel * m_00
    s_xx = m_20 - 2.0 * u_rel * m_10 + u_rel * u_rel * m_00
    s_xy = m_11 - u_rel * m_01 - w_rel * m_10 + u_rel * w_rel * m_00
    s_yy = m_02 - 2.0 * w_rel * m_01 + w_rel * w_rel * m_00
    by_det = -(coef_a * s_xx + coef_b * s_xy + coef_c * s_yy) * inv_det
    derivs = [
        -(2.0 * coef_a * s_x + coef_b * s_y),
        -(2.0 * coef_c * s_y + coef_b * s_x),
        -0.5 * inv_det * s_yy + by_det * c_c,
        inv_det * s_xy - 2.0 * c_b * by_det,
        -0.5 * inv_det * s_xx + by_det * c_a,
        m_00 / opac,
    ] + [exact_dot(power[0:tiles], moment_s[3 + ch], NT) for ch in range(3)]
    for p in range(ROW_REC):
        split_pairs = jnp.concatenate(
            [derivs[p][:, k * block_len : (k + 1) * block_len] for k in range(TILE_MOST)], axis=0
        )
        routed = exact_dot(put_owner, split_pairs, NN)
        for h in range(halves):
            grad_out[:, p * halves + h, :] = routed[:, h * 128 : (h + 1) * 128]
    grad_out[:, ROW_REC * halves, :] = jnp.broadcast_to(loss, (devices, 128))
    to_all(lambda peer: grad_out.at[peer], grad_in, 2)
    grad_in[me] = grad_out[me]
    wait_all(grad_in, 2)
    incoming_ref[...] = grad_in[...]


def adam_kernel(
    geometry,
    messages_ref,
    incoming_ref,
    rates_ref,
    gauss_ref,
    one_ref,
    two_ref,
    out_gauss,
    out_one,
    out_two,
    out_loss,
    out_grad_hbm,
    out_grad,
    one_v,
    two_v,
    gauss_v,
    read_sem,
    write_sem,
):
    fetch_one = pltpu.make_async_copy(one_ref, one_v, read_sem.at[0])
    fetch_two = pltpu.make_async_copy(two_ref, two_v, read_sem.at[1])
    fetch_one.start()
    fetch_two.start()
    views_n, bands_n, blocks, list_len, rows, cols, block_len = geometry
    devices = views_n * bands_n
    halves = block_len // 128
    me = lax.axis_index("view") * bands_n + lax.axis_index("band")
    base = (me * blocks).astype(F32)
    asked = messages_ref[...]
    hot = requests_of(asked, base, list_len, blocks)
    missing = 1.0 - jnp.max(hot, axis=1, keepdims=True)
    cam = [asked[:, c : c + 1] for c in range(9)]

    def picked(component):
        return exact_dot(hot, gauss_ref[component], NN)

    def arrived(p):
        return jnp.concatenate(
            [incoming_ref[:, p * halves + h, :] for h in range(halves)], axis=1
        )

    d_u, d_w = arrived(0), arrived(1)
    columns = []
    along = [cam[c] * d_u + cam[3 + c] * d_w for c in range(3)]
    columns += along + [cam[8] * value for value in along]
    quats = [picked(9 + c) for c in range(4)]
    quats[0] = quats[0] + missing
    logs = [picked(6 + c) for c in range(3)]
    _, pullback = jax.vjp(
        lambda a, b, c: shape_of(cam[0:6], a, b, c), logs, quats, picked(13)
    )
    d_logs, d_quats, d_logit = pullback(tuple(arrived(2 + p) for p in range(4)))
    columns += list(d_logs) + list(d_quats) + [d_logit]
    turned = jnp.transpose(jnp.concatenate([asked] * 3, axis=0))
    hot_t = jnp.transpose(hot)
    for c in range(14):
        out_grad[c] = exact_dot(hot_t, columns[c], NN)
    basis = camera_basis([turned[c : c + 1, :] for c in range(6)])
    channel = lax.broadcasted_iota(jnp.int32, (3, 3 * devices), 1) // devices
    own_channel = channel == lax.broadcasted_iota(jnp.int32, (3, 3 * devices), 0)
    fan = jnp.concatenate([jnp.where(own_channel, value, 0.0) for value in basis], axis=0)
    hot_3 = jnp.transpose(jnp.concatenate([hot] * 3, axis=0))
    shades = fan.shape[0]
    routed = jnp.concatenate([hot_3 * fan[r : r + 1, :] for r in range(shades)], axis=0)
    tinted = jnp.concatenate([arrived(6 + ch) for ch in range(3)], axis=0)
    colour = jnp.dot(routed, tinted, precision=HIGHEST_MODE, preferred_element_type=F32)
    for r in range(shades):
        out_grad[14 + r] = colour[r * blocks : (r + 1) * blocks]
    losses = incoming_ref[:, ROW_REC * halves, :]
    out_loss[...] = jnp.sum(losses, axis=0, keepdims=True)[:, 0:1] * (
        1.0 / (devices * rows * cols)
    )
    fetch_one.wait()
    fetch_two.wait()
    comps = gauss_ref.shape[0]
    pieces = []
    for piece in range(PIECES):
        low, high = piece * comps // PIECES, (piece + 1) * comps // PIECES

        def update(c, carry):
            gradient = out_grad[c]
            new_one = 0.9 * one_v[c] + 0.1 * gradient
            new_two = 0.999 * two_v[c] + 0.001 * gradient * gradient
            one_v[c] = new_one
            two_v[c] = new_two
            bottom = jnp.sqrt(new_two * (1.0 / BIAS_SECOND)) + 1e-08
            gauss_v[c] = gauss_ref[c] - rates_ref[c] * new_one / bottom
            return carry

        lax.fori_loop(low, high, update, 0, unroll=2)
        part = pl.ds(low, high - low)
        for source, landing, sem in (
            (one_v, out_one, 0),
            (two_v, out_two, 1),
            (gauss_v, out_gauss, 2),
            (out_grad, out_grad_hbm, 3),
        ):
            copy = pltpu.make_async_copy(
                source.at[part], landing.at[part], write_sem.at[sem, piece]
            )
            copy.start()
            pieces.append(copy)
    for copy in pieces:
        copy.wait()


def per_device(
    gaussians,
    first_moment,
    second_moment,
    camera,
    target,
    block_list,
    block_count,
    tile_start,
    tile_end,
):
    views_n = lax.axis_size("view")
    bands_n = lax.axis_size("band")
    devices = views_n * bands_n
    blocks, comps, block_len = gaussians.shape
    list_len = block_list.shape[2]
    rows, cols = target.shape[2:]
    tiles = cols // TILE
    pairs = TILE_MOST * tiles
    halves = block_len // 128
    geometry = (views_n, bands_n, blocks, list_len, rows, cols, block_len)

    message = jnp.concatenate(
        [
            camera,
            jnp.zeros((1, 7), F32),
            block_list[0].astype(F32),
            jnp.zeros((1, 128 - 16 - list_len), F32),
        ],
        axis=1,
    )
    spot = tile_start[0, 0][None, :] + jnp.arange(TILE_MOST, dtype=jnp.int32)[:, None]
    spot = jnp.where(spot < tile_end[0, 0][None, :], spot, -1).reshape(pairs, 1)
    place = (spot == jnp.arange(128, dtype=jnp.int32)[None, :]).astype(F32)
    table = jnp.concatenate([message, place], axis=0)[:, None, :]

    across, first, second = smoothing_tables(rows, cols, 3)
    power = power_table(tiles, cols)
    vmem = pl.BlockSpec(memory_space=pltpu.VMEM)
    hbm = pl.BlockSpec(memory_space=pl.ANY)

    def by_comp(array):
        return jnp.transpose(array, (1, 0, 2))

    rec_rows = ROW_REC * halves
    window = TILE_MOST * block_len
    incoming, messages = pl.pallas_call(
        functools.partial(step_kernel, geometry),
        out_shape=(
            jax.ShapeDtypeStruct((devices, rec_rows + 1, 128), F32),
            jax.ShapeDtypeStruct((devices, 128), F32),
        ),
        in_specs=[vmem] * 7,
        out_specs=(vmem, vmem),
        scratch_shapes=[
            pltpu.VMEM((devices, 1, 128), F32),
            pltpu.VMEM((devices, rec_rows, 128), F32),
            pltpu.VMEM((devices, rec_rows, 128), F32),
            pltpu.VMEM((devices, rec_rows + 1, 128), F32),
            pltpu.VMEM((devices, rec_rows + 1, 128), F32),
            pltpu.VMEM((2, 3, REACH, cols), F32),
            pltpu.VMEM((2, 3, REACH, cols), F32),
            pltpu.VMEM((2, 3, REACH, cols), F32),
            pltpu.VMEM((2, 3, REACH, cols), F32),
            pltpu.VMEM((6, window, cols), F32),
            pltpu.VMEM((window, rows // 8, 8, cols), F32),
            pltpu.VMEM((window, rows // 8, 8, cols), F32),
            pltpu.VMEM((6, window, cols), F32),
            pltpu.SemaphoreType.DMA((3,)),
            pltpu.SemaphoreType.DMA((3,)),
            pltpu.SemaphoreType.DMA((2, 2)),
            pltpu.SemaphoreType.DMA((2, 2)),
        ],
        compiler_params=pltpu.CompilerParams(collective_id=0, has_side_effects=True),
        name="render_step",
    )(table, target, by_comp(gaussians), across, first, second, power)

    rates = learning_rates() / BIAS_FIRST
    shape = jax.ShapeDtypeStruct((comps, blocks, block_len), F32)
    new_params, new_one, new_two, mean_loss, gradient = pl.pallas_call(
        functools.partial(adam_kernel, geometry),
        out_shape=(shape, shape, shape, jax.ShapeDtypeStruct((1, 1), F32), shape),
        in_specs=[vmem, vmem, pl.BlockSpec(memory_space=pltpu.SMEM), vmem, hbm, hbm],
        out_specs=(hbm, hbm, hbm, vmem, hbm),
        scratch_shapes=[pltpu.VMEM((comps, blocks, block_len), F32)] * 4
        + [pltpu.SemaphoreType.DMA((2,)), pltpu.SemaphoreType.DMA((4, PIECES))],
        name="adam_step",
    )(
        messages,
        incoming,
        rates,
        by_comp(gaussians),
        by_comp(first_moment),
        by_comp(second_moment),
    )
    return (
        by_comp(new_params),
        by_comp(new_one),
        by_comp(new_two),
        mean_loss.reshape(()),
        by_comp(gradient),
    )


def solution(mesh):
    return jax.shard_map(
        per_device,
        mesh=mesh,
        in_specs=(
            P(("view", "band"), None, None),
            P(("view", "band"), None, None),
            P(("view", "band"), None, None),
            P("view", None),
            P("view", None, "band", None),
            P("view", "band", None),
            P("view", "band"),
            P("view", "band", None),
            P("view", "band", None),
        ),
        out_specs=(
            P(("view", "band"), None, None),
            P(("view", "band"), None, None),
            P(("view", "band"), None, None),
            P(),
            P(("view", "band"), None, None),
        ),
        check_vma=False,
    )
```

```python
import functools
import math

import jax
import jax.numpy as jnp
import numpy as np
from jax import lax
from jax.experimental import pallas as pl
from jax.experimental.pallas import tpu as pltpu
from jax.sharding import PartitionSpec as P

TILE = 16
TILE_MOST = 2
HALO = 5
REACH = 2 * HALO
ROW_REC = 9
GEO_REC = 6
PIECES = 4

HIGHEST_MODE = lax.Precision.HIGHEST
SSIM_WEIGHT = 0.2
ABS_WEIGHT = 0.8
STAB_MEAN = 0.0001
STAB_VAR = 0.0009
BIAS_FIRST = 1.0 - math.exp(100.0 * math.log(0.9))
BIAS_SECOND = 1.0 - math.exp(100.0 * math.log(0.999))
LOG2_E = math.log2(math.e)
SH_ZERO = 0.28209479177387814
SH_ONE = 0.4886025119029199
SH_TWO = [
    1.0925484305920792,
    -1.0925484305920792,
    0.31539156525252005,
    -1.0925484305920792,
    0.5462742152960396,
]
SH_THREE = [
    -0.5900435899266435,
    2.890611442640554,
    -0.4570457994644658,
    0.3731763325901154,
    -0.4570457994644658,
    1.445305721320277,
    -0.5900435899266435,
]
F32 = jnp.float32
BF16 = jnp.bfloat16
MESH = pl.DeviceIdType.MESH
NEVER = -1e30


def learning_rates():
    return np.concatenate(
        [
            np.full(6, 0.016),
            np.full(3, 0.005),
            np.full(4, 0.001),
            np.full(1, 0.05),
            np.full(3, 0.0025),
            np.full(45, 0.000125),
        ]
    ).astype(np.float32)


def kernel_taps():
    raw_taps = [math.exp(-(offset * offset) / 4.5) for offset in range(-5, 6)]
    tap_total = sum(raw_taps)
    return [raw_tap / tap_total for raw_tap in raw_taps]


def up8(value):
    return (value + 7) // 8 * 8


def smoothing_tables(rows, cols, channels):
    taps = kernel_taps()
    in_rows, mid_rows = up8(rows + 2 * REACH), up8(rows + REACH)
    across = np.zeros((cols, cols), np.float32)
    for out in range(cols):
        for m in range(-HALO, HALO + 1):
            if 0 <= out + m < cols:
                across[out + m, out] = taps[m + HALO]
    first = np.zeros((channels * mid_rows, channels * in_rows), np.float32)
    second = np.zeros((channels * rows, channels * mid_rows), np.float32)
    for c in range(channels):
        for e in range(rows + REACH):
            for m in range(REACH + 1):
                first[c * mid_rows + e, c * in_rows + e + m] = taps[m]
        for i in range(rows):
            for m in range(REACH + 1):
                second[c * rows + i, c * mid_rows + i + m] = taps[m]
    return across, first, second


def power_table(tiles, cols):
    lane = np.arange(cols)
    local = lane % TILE + 0.5 - TILE / 2
    belongs = (lane[None, :] // TILE == np.arange(tiles)[:, None]).astype(np.float32)
    return np.concatenate([belongs, belongs * local, belongs * local * local]).astype(np.float32)


def harmonics(dir_x, dir_y, dir_z):
    sq_x, sq_y, sq_z = (dir_x * dir_x, dir_y * dir_y, dir_z * dir_z)
    return [
        SH_ZERO + 0.0 * dir_x,
        -SH_ONE * dir_y,
        SH_ONE * dir_z,
        -SH_ONE * dir_x,
        SH_TWO[0] * dir_x * dir_y,
        SH_TWO[1] * dir_y * dir_z,
        SH_TWO[2] * (2.0 * sq_z - sq_x - sq_y),
        SH_TWO[3] * dir_x * dir_z,
        SH_TWO[4] * (sq_x - sq_y),
        SH_THREE[0] * dir_y * (3.0 * sq_x - sq_y),
        SH_THREE[1] * dir_x * dir_y * dir_z,
        SH_THREE[2] * dir_y * (4.0 * sq_z - sq_x - sq_y),
        SH_THREE[3] * dir_z * (2.0 * sq_z - 3.0 * sq_x - 3.0 * sq_y),
        SH_THREE[4] * dir_x * (4.0 * sq_z - sq_x - sq_y),
        SH_THREE[5] * dir_z * (sq_x - sq_y),
        SH_THREE[6] * dir_x * (sq_x - 3.0 * sq_y),
    ]


def camera_basis(affine):
    a, b = affine[0:3], affine[3:6]
    n_x = a[1] * b[2] - a[2] * b[1]
    n_y = a[2] * b[0] - a[0] * b[2]
    n_z = a[0] * b[1] - a[1] * b[0]
    length = jnp.sqrt(n_x * n_x + n_y * n_y + n_z * n_z)
    return harmonics(n_x / length, n_y / length, n_z / length)


def shape_of(affine, logs, quats, logit):
    scales = [jnp.exp(value) for value in logs]
    quat_len = jnp.sqrt(
        quats[0] * quats[0] + quats[1] * quats[1] + quats[2] * quats[2] + quats[3] * quats[3]
    )
    r, i, j, k = [value / quat_len for value in quats]
    rotation = [
        [1.0 - 2.0 * (j * j + k * k), 2.0 * (i * j - r * k), 2.0 * (i * k + r * j)],
        [2.0 * (i * j + r * k), 1.0 - 2.0 * (i * i + k * k), 2.0 * (j * k - r * i)],
        [2.0 * (i * k - r * j), 2.0 * (j * k + r * i), 1.0 - 2.0 * (i * i + j * j)],
    ]
    m = [
        [
            (
                affine[3 * o] * rotation[0][c]
                + affine[3 * o + 1] * rotation[1][c]
                + affine[3 * o + 2] * rotation[2][c]
            )
            * scales[c]
            for c in range(3)
        ]
        for o in range(2)
    ]
    conic_a = m[0][0] * m[0][0] + m[0][1] * m[0][1] + m[0][2] * m[0][2] + 0.3
    conic_b = m[0][0] * m[1][0] + m[0][1] * m[1][1] + m[0][2] * m[1][2]
    conic_c = m[1][0] * m[1][0] + m[1][1] * m[1][1] + m[1][2] * m[1][2] + 0.3
    opacity = 1.0 / (1.0 + jnp.exp(-logit))
    return conic_a, conic_b, conic_c, opacity


def split3(value, axis=0):
    high = value.astype(BF16)
    rest = value - high.astype(F32)
    middle = rest.astype(BF16)
    low = (rest - middle.astype(F32)).astype(BF16)
    return high, middle, low


def exact_dot(table, value, dims):
    table = table.astype(BF16)
    total = None
    for part in split3(value):
        term = lax.dot_general(table, part, (dims, ((), ())), preferred_element_type=F32)
        total = term if total is None else total + term
    return total


def expand_dot(value, table):
    table = table.astype(BF16)
    total = None
    for part in split3(value):
        term = lax.dot_general(
            part, table, (((0,), (0,)), ((), ())), preferred_element_type=F32
        )
        total = term if total is None else total + term
    return total


NN = ((1,), (0,))
NT = ((1,), (1,))


def requests_of(messages, base, list_len, blocks):
    devices = messages.shape[0]
    block_iota = lax.broadcasted_iota(jnp.int32, (devices, blocks), 1).astype(F32) + base
    hit = jnp.zeros((devices, blocks), F32)
    for i in range(list_len):
        wanted = messages[:, 16 + i : 17 + i]
        hit = hit + jnp.where(wanted == block_iota, 1.0, 0.0)
    return hit


def tree_sum(vregs, lane_count):
    sub = lax.broadcasted_iota(jnp.int32, (8, lane_count), 0)

    def join(a, b, mask, shift):
        return jnp.where(mask, a, b) + pltpu.roll(jnp.where(mask, b, a), 8 - shift, 0)

    def half(offset):
        return ((sub + (8 - offset)) % 8) < 4

    def quarter(offset):
        return ((sub + (8 - offset)) % 4) < 2

    z1 = join(
        join(vregs[0], vregs[4], half(0), 4), join(vregs[2], vregs[6], half(2), 4), quarter(0), 2
    )
    z2 = join(
        join(vregs[1], vregs[5], half(1), 4), join(vregs[3], vregs[7], half(3), 4), quarter(1), 2
    )
    return join(z1, z2, (sub % 2) < 1, 1)


def step_kernel(
    geometry,
    camera_ref,
    list_ref,
    start_ref,
    end_ref,
    target_ref,
    gauss_hbm,
    across_ref,
    first_ref,
    second_ref,
    power_ref,
    incoming_ref,
    messages_ref,
    gauss_ref,
    msg_out,
    msg_in,
    geo_out,
    geo_in,
    tint_out,
    tint_in,
    grad_out,
    grad_in,
    halo_out,
    halo_in,
    thalo_out,
    thalo_in,
    coef,
    alpha_s,
    trans_s,
    moment_s,
    send_sem,
    recv_sem,
    halo_send,
    halo_recv,
    fetch_sem,
):
    views_n, bands_n, blocks, list_len, rows, cols, block_len = geometry
    devices = views_n * bands_n
    tiles = cols // TILE
    pairs = TILE_MOST * tiles
    window = TILE_MOST * block_len
    halves = block_len // 128
    view = lax.axis_index("view")
    band = lax.axis_index("band")
    me = view * bands_n + band
    base = (me * blocks).astype(F32)
    has_up = band > 0
    has_down = band < bands_n - 1

    def peer_of(d):
        return (lax.rem(view + d, views_n), lax.rem(band + d // views_n, bands_n))

    fetch = pltpu.make_async_copy(gauss_hbm, gauss_ref, fetch_sem.at[0])
    fetch.start()

    msg_out[...] = jnp.zeros_like(msg_out)
    msg_out[:, 0:9] = camera_ref[...]
    list_row = list_ref[0].astype(F32)
    msg_out[:, 16 : 16 + list_len] = list_row
    halo_in[...] = jnp.zeros_like(halo_in)
    thalo_in[...] = jnp.zeros_like(thalo_in)
    thalo_out[0] = target_ref[0, :, 0:REACH, :]
    thalo_out[1] = target_ref[0, :, rows - REACH : rows, :]
    barrier = pltpu.get_barrier_semaphore()

    def greet(d, carry):
        pl.semaphore_signal(barrier, inc=1, device_id=peer_of(d), device_id_type=MESH)
        return carry

    lax.fori_loop(1, devices, greet, 0)
    pl.semaphore_wait(barrier, devices - 1)

    def to_all(source_of, landing, phase):
        def send(d, carry):
            peer_view, peer_band = peer_of(d)
            peer = peer_view * bands_n + peer_band
            pltpu.make_async_remote_copy(
                src_ref=source_of(peer),
                dst_ref=landing.at[me],
                send_sem=send_sem.at[phase],
                recv_sem=recv_sem.at[phase],
                device_id=peer_of(d),
                device_id_type=MESH,
            ).start()
            return carry

        lax.fori_loop(1, devices, send, 0)

    def wait_all(landing, phase):
        every = landing.at[pl.ds(0, devices - 1)]
        pltpu.make_async_copy(every, every, recv_sem.at[phase]).wait()
        pltpu.make_async_copy(every, every, send_sem.at[phase]).wait()

    def edge_copy(source, landing, direction, phase):
        step = -1 if direction == 0 else 1
        return pltpu.make_async_remote_copy(
            src_ref=source.at[direction],
            dst_ref=landing.at[1 - direction],
            send_sem=halo_send.at[phase, direction],
            recv_sem=halo_recv.at[phase, 1 - direction],
            device_id=(view, band + step),
            device_id_type=MESH,
        )

    def edges_start(source, landing, phase):
        @pl.when(has_up)
        def _():
            edge_copy(source, landing, 0, phase).start()

        @pl.when(has_down)
        def _():
            edge_copy(source, landing, 1, phase).start()

    def edges_wait(source, landing, phase):
        @pl.when(has_up)
        def _():
            up = edge_copy(source, landing, 0, phase)
            up.wait_send()
            pltpu.make_async_copy(
                landing.at[0], landing.at[0], halo_recv.at[phase, 0]
            ).wait()

        @pl.when(has_down)
        def _():
            down = edge_copy(source, landing, 1, phase)
            down.wait_send()
            pltpu.make_async_copy(
                landing.at[1], landing.at[1], halo_recv.at[phase, 1]
            ).wait()

    to_all(lambda peer: msg_out, msg_in, 0)
    edges_start(thalo_out, thalo_in, 0)
    msg_in[me] = msg_out[...]

    owner_low = lax.broadcasted_iota(jnp.int32, (devices, list_len), 0).astype(F32) * blocks
    owner_hot = jnp.where((list_row >= owner_low) & (list_row < owner_low + blocks), 1.0, 0.0)
    pair_row = lax.broadcasted_iota(jnp.int32, (pairs, tiles), 0)
    on_tile = pair_row % tiles == lax.broadcasted_iota(jnp.int32, (pairs, tiles), 1)

    def upright(row):
        return jnp.sum(jnp.where(on_tile, row.astype(F32), 0.0), axis=1, keepdims=True)

    later = (lax.broadcasted_iota(jnp.int32, (pairs, 1), 0) // tiles).astype(F32)
    spot = upright(start_ref[0]) + later
    position = lax.broadcasted_iota(jnp.int32, (pairs, list_len), 1).astype(F32)
    place = jnp.where((position == spot) & (spot < upright(end_ref[0])), 1.0, 0.0)
    live_pair = jnp.max(place, axis=1, keepdims=True)
    pick_owner = lax.dot_general(
        place.astype(BF16), owner_hot.astype(BF16), (NT, ((), ())), preferred_element_type=F32
    )
    put_owner = lax.dot_general(
        owner_hot.astype(BF16), place.astype(BF16), (NT, ((), ())), preferred_element_type=F32
    )
    live = jnp.concatenate(
        [
            jnp.broadcast_to(live_pair[k * tiles : (k + 1) * tiles], (tiles, block_len))
            for k in range(TILE_MOST)
        ],
        axis=1,
    )

    wait_all(msg_in, 0)
    fetch.wait()

    asked = msg_in[...].reshape(devices, 128)
    messages_ref[...] = asked
    hot = requests_of(asked, base, list_len, blocks)
    missing = 1.0 - jnp.max(hot, axis=1, keepdims=True)
    cam = [asked[:, c : c + 1] for c in range(9)]

    def picked(component):
        return exact_dot(hot, gauss_ref[component], NN)

    centre = [picked(c) + cam[8] * picked(3 + c) for c in range(3)]
    records = [
        cam[0] * centre[0] + cam[1] * centre[1] + cam[2] * centre[2] + cam[6],
        cam[3] * centre[0] + cam[4] * centre[1] + cam[5] * centre[2] + cam[7],
    ]
    quats = [picked(9 + c) for c in range(4)]
    quats[0] = quats[0] + missing
    conic_a, conic_b, conic_c, opacity = shape_of(
        cam[0:6], [picked(6 + c) for c in range(3)], quats, picked(13)
    )
    records += [conic_a, conic_b, conic_c, opacity]
    for p in range(GEO_REC):
        for h in range(halves):
            geo_out[:, p * halves + h, :] = records[p][:, h * 128 : (h + 1) * 128]
    to_all(lambda peer: geo_out.at[peer], geo_in, 1)
    geo_in[me] = geo_out[me]
    basis = camera_basis(cam)
    basis = [jnp.where(missing > 0.5, 0.0, value) for value in basis]
    for ch in range(3):
        colour = 0.5
        for q in range(16):
            colour = colour + basis[q] * picked(14 + 3 * q + ch)
        for h in range(halves):
            tint_out[:, ch * halves + h, :] = colour[:, h * 128 : (h + 1) * 128]
    to_all(lambda peer: tint_out.at[peer], tint_in, 2)
    tint_in[me] = tint_out[me]
    wait_all(geo_in, 1)

    def gathered(landed, p):
        parts = []
        for h in range(halves):
            parts.append(exact_dot(pick_owner, landed[:, p * halves + h, :], NN))
        whole = jnp.concatenate(parts, axis=1)
        return jnp.concatenate(
            [whole[k * tiles : (k + 1) * tiles] for k in range(TILE_MOST)], axis=1
        )

    dead = 1.0 - live
    tile_row = lax.broadcasted_iota(jnp.int32, (tiles, window), 0).astype(F32)
    u_rel = gathered(geo_in, 0) - (tile_row * TILE + 0.5 * TILE)
    w_rel = gathered(geo_in, 1) - ((band * rows).astype(F32) + 0.5 * TILE)
    c_a = gathered(geo_in, 2) + dead
    c_b = gathered(geo_in, 3)
    c_c = gathered(geo_in, 4) + dead
    opac = gathered(geo_in, 5) + dead
    inv_det = 1.0 / (c_a * c_c - c_b * c_b)
    coef_a = -0.5 * c_c * inv_det
    coef_b = c_b * inv_det
    coef_c = -0.5 * c_a * inv_det
    keep = live > 0.5

    def masked(value, other=0.0):
        return jnp.where(keep, value, other)

    flat = LOG2_E * (
        coef_a * u_rel * u_rel + coef_b * u_rel * w_rel + coef_c * w_rel * w_rel
    ) + LOG2_E * jnp.log(opac)
    power = power_ref[...]
    coef[0] = expand_dot(
        jnp.concatenate(
            [
                masked(flat, NEVER),
                masked(LOG2_E * (-2.0 * coef_a * u_rel - coef_b * w_rel)),
                masked(LOG2_E * coef_a),
            ],
            axis=0,
        ),
        power,
    )
    coef[1] = expand_dot(
        jnp.concatenate(
            [
                masked(LOG2_E * (-coef_b * u_rel - 2.0 * coef_c * w_rel)),
                masked(LOG2_E * coef_b),
            ],
            axis=0,
        ),
        power[0 : 2 * tiles],
    )
    coef[2] = expand_dot(masked(LOG2_E * coef_c), power[0:tiles])
    wait_all(tint_in, 2)
    for ch in range(3):
        coef[3 + ch] = expand_dot(masked(gathered(tint_in, ch)), power[0:tiles])

    sub8 = lax.broadcasted_iota(jnp.int32, (8, cols), 0).astype(F32)
    parts_n = rows // 8
    row_local = [sub8 + (8.0 * part + 0.5 - 0.5 * TILE) for part in range(parts_n)]

    def spread_row(kind, j):
        return coef[kind, pl.ds(j, 8, stride=0), :]

    def blend(group, carry):
        trans, image = carry
        trans, image = list(trans), list(image)
        for k in range(8):
            j = group * 8 + k
            q0, q1, q2 = spread_row(0, j), spread_row(1, j), spread_row(2, j)
            tint = [spread_row(3 + ch, j) for ch in range(3)]
            for part in range(parts_n):
                r = row_local[part]
                alpha = jnp.exp2(q0 + r * (q1 + r * q2))
                weight = alpha * trans[part]
                alpha_s[j, part] = alpha
                trans_s[j, part] = trans[part]
                trans[part] = trans[part] - weight
                for ch in range(3):
                    at = ch * parts_n + part
                    image[at] = image[at] + weight * tint[ch]
        return tuple(trans), tuple(image)

    zero = jnp.zeros((8, cols), F32)
    _, image = lax.fori_loop(
        0,
        window // 8,
        blend,
        (tuple([zero + 1.0] * parts_n), tuple([zero] * (3 * parts_n))),
    )
    pred = [
        jnp.concatenate([image[ch * parts_n + part] for part in range(parts_n)], axis=0)
        for ch in range(3)
    ]
    for ch in range(3):
        halo_out[0, ch] = pred[ch][0:REACH]
        halo_out[1, ch] = pred[ch][rows - REACH : rows]
    edges_start(halo_out, halo_in, 1)
    edges_wait(thalo_out, thalo_in, 0)
    edges_wait(halo_out, halo_in, 1)

    in_rows, mid_rows = up8(rows + 2 * REACH), up8(rows + REACH)
    fill = jnp.zeros((in_rows - rows - 2 * REACH, cols), F32)
    mine = target_ref[0]
    ext_x = jnp.concatenate(
        [v for ch in range(3) for v in (halo_in[0, ch], pred[ch], halo_in[1, ch], fill)], axis=0
    )
    ext_y = jnp.concatenate(
        [v for ch in range(3) for v in (thalo_in[0, ch], mine[ch], thalo_in[1, ch], fill)], axis=0
    )
    fields = jnp.concatenate(
        [ext_x, ext_y, ext_x * ext_x, ext_y * ext_y, ext_x * ext_y], axis=1
    )
    down = jnp.dot(first_ref[...], fields, precision=HIGHEST_MODE, preferred_element_type=F32)
    stacked = jnp.concatenate([down[:, f * cols : (f + 1) * cols] for f in range(5)], axis=0)
    smoothed = jnp.dot(
        stacked, across_ref[...], precision=HIGHEST_MODE, preferred_element_type=F32
    )
    high = 3 * mid_rows
    mean_x, mean_y, square_x, square_y, cross = [
        smoothed[f * high : (f + 1) * high] for f in range(5)
    ]
    n_mean = 2.0 * mean_x * mean_y + STAB_MEAN
    n_var = 2.0 * (cross - mean_x * mean_y) + STAB_VAR
    d_mean = mean_x * mean_x + mean_y * mean_y + STAB_MEAN
    d_var = (square_x - mean_x * mean_x) + (square_y - mean_y * mean_y) + STAB_VAR
    inv_mean = 1.0 / d_mean
    inv_var = 1.0 / d_var
    inverse = inv_mean * inv_var
    ssim = n_mean * n_var * inverse
    ext_row = lax.broadcasted_iota(jnp.int32, (high, cols), 0) % mid_rows
    image_row = ext_row + (band * rows - HALO)
    inside = (image_row >= 0) & (image_row < bands_n * rows) & (ext_row < rows + REACH)
    scale = -SSIM_WEIGHT / 3.0
    part_mean = 2.0 * mean_y * (n_var - n_mean) * inverse - 2.0 * mean_x * ssim * (
        inv_mean - inv_var
    )
    adjoint = jnp.concatenate(
        [
            jnp.where(inside, scale * part_mean, 0.0),
            jnp.where(inside, -scale * ssim * inv_var, 0.0),
            jnp.where(inside, (2.0 * scale) * n_mean * inverse, 0.0),
        ],
        axis=1,
    )
    down2 = jnp.dot(second_ref[...], adjoint, precision=HIGHEST_MODE, preferred_element_type=F32)
    stacked2 = jnp.concatenate([down2[:, f * cols : (f + 1) * cols] for f in range(3)], axis=0)
    spread = jnp.dot(
        stacked2, across_ref[...], precision=HIGHEST_MODE, preferred_element_type=F32
    )
    deep = 3 * rows
    pred_all = jnp.concatenate(pred, axis=0)
    mine_all = jnp.concatenate([mine[ch] for ch in range(3)], axis=0)
    error = pred_all - mine_all
    sign = jnp.where(error > 0.0, 1.0, jnp.where(error < 0.0, -1.0, 0.0))
    grad_pred = (
        ABS_WEIGHT / 3.0 * sign
        + spread[0:deep]
        + 2.0 * pred_all * spread[deep : 2 * deep]
        + mine_all * spread[2 * deep : 3 * deep]
    )
    own = (ext_row >= HALO) & (ext_row < HALO + rows)
    loss = jnp.sum(ABS_WEIGHT / 3.0 * jnp.abs(error), keepdims=True) + jnp.sum(
        jnp.where(own, SSIM_WEIGHT / 3.0 * (1.0 - ssim), 0.0), keepdims=True
    )

    pull = [
        [grad_pred[ch * rows + 8 * part : ch * rows + 8 * part + 8] for part in range(parts_n)]
        for ch in range(3)
    ]

    def unblend(step, behind):
        group = window // 8 - 1 - step
        behind = list(behind)
        sums = [[None] * 8 for _ in range(6)]
        for k in reversed(range(8)):
            j = group * 8 + k
            tint = [spread_row(3 + ch, j) for ch in range(3)]
            totals = [None] * 6
            for part in range(parts_n):
                alpha = alpha_s[j, part]
                trans = trans_s[j, part]
                shade = (
                    tint[0] * pull[0][part] + tint[1] * pull[1][part] + tint[2] * pull[2][part]
                )
                gap = shade - behind[part]
                behind[part] = behind[part] + alpha * gap
                weight = alpha * trans
                lean = weight * gap
                lean_r = lean * row_local[part]
                terms = [lean, lean_r, lean_r * row_local[part]]
                terms += [weight * pull[ch][part] for ch in range(3)]
                totals = [
                    term if total is None else total + term for term, total in zip(terms, totals)
                ]
            for kind in range(6):
                sums[kind][k] = totals[kind]
        at = pl.multiple_of(group * 8, 8)
        for kind in range(6):
            moment_s[kind, pl.ds(at, 8), :] = tree_sum(sums[kind], cols)
        return tuple(behind)

    lax.fori_loop(0, window // 8, unblend, tuple([zero] * parts_n))

    by_x = exact_dot(power, moment_s[0], NT)
    m_00, m_10, m_20 = by_x[0:tiles], by_x[tiles : 2 * tiles], by_x[2 * tiles : 3 * tiles]
    by_xr = exact_dot(power[0 : 2 * tiles], moment_s[1], NT)
    m_01, m_11 = by_xr[0:tiles], by_xr[tiles : 2 * tiles]
    m_02 = exact_dot(power[0:tiles], moment_s[2], NT)
    s_x = m_10 - u_rel * m_00
    s_y = m_01 - w_rel * m_00
    s_xx = m_20 - 2.0 * u_rel * m_10 + u_rel * u_rel * m_00
    s_xy = m_11 - u_rel * m_01 - w_rel * m_10 + u_rel * w_rel * m_00
    s_yy = m_02 - 2.0 * w_rel * m_01 + w_rel * w_rel * m_00
    by_det = -(coef_a * s_xx + coef_b * s_xy + coef_c * s_yy) * inv_det
    derivs = [
        -(2.0 * coef_a * s_x + coef_b * s_y),
        -(2.0 * coef_c * s_y + coef_b * s_x),
        -0.5 * inv_det * s_yy + by_det * c_c,
        inv_det * s_xy - 2.0 * c_b * by_det,
        -0.5 * inv_det * s_xx + by_det * c_a,
        m_00 / opac,
    ] + [exact_dot(power[0:tiles], moment_s[3 + ch], NT) for ch in range(3)]
    for p in range(ROW_REC):
        split_pairs = jnp.concatenate(
            [derivs[p][:, k * block_len : (k + 1) * block_len] for k in range(TILE_MOST)], axis=0
        )
        routed = exact_dot(put_owner, split_pairs, NN)
        for h in range(halves):
            grad_out[:, p * halves + h, :] = routed[:, h * 128 : (h + 1) * 128]
    grad_out[:, ROW_REC * halves, :] = jnp.broadcast_to(loss, (devices, 128))
    to_all(lambda peer: grad_out.at[peer], grad_in, 3)
    grad_in[me] = grad_out[me]
    wait_all(grad_in, 3)
    incoming_ref[...] = grad_in[...]


def adam_kernel(
    geometry,
    messages_ref,
    incoming_ref,
    rates_ref,
    gauss_ref,
    one_ref,
    two_ref,
    out_gauss,
    out_one,
    out_two,
    out_loss,
    out_grad_hbm,
    out_grad,
    one_v,
    two_v,
    gauss_v,
    read_sem,
    write_sem,
):
    fetch_one = pltpu.make_async_copy(one_ref, one_v, read_sem.at[0])
    fetch_two = pltpu.make_async_copy(two_ref, two_v, read_sem.at[1])
    fetch_one.start()
    fetch_two.start()
    views_n, bands_n, blocks, list_len, rows, cols, block_len = geometry
    devices = views_n * bands_n
    halves = block_len // 128
    me = lax.axis_index("view") * bands_n + lax.axis_index("band")
    base = (me * blocks).astype(F32)
    asked = messages_ref[...]
    hot = requests_of(asked, base, list_len, blocks)
    missing = 1.0 - jnp.max(hot, axis=1, keepdims=True)
    cam = [asked[:, c : c + 1] for c in range(9)]

    def picked(component):
        return exact_dot(hot, gauss_ref[component], NN)

    def arrived(p):
        return jnp.concatenate(
            [incoming_ref[:, p * halves + h, :] for h in range(halves)], axis=1
        )

    d_u, d_w = arrived(0), arrived(1)
    columns = []
    along = [cam[c] * d_u + cam[3 + c] * d_w for c in range(3)]
    columns += along + [cam[8] * value for value in along]
    quats = [picked(9 + c) for c in range(4)]
    quats[0] = quats[0] + missing
    logs = [picked(6 + c) for c in range(3)]
    _, pullback = jax.vjp(
        lambda a, b, c: shape_of(cam[0:6], a, b, c), logs, quats, picked(13)
    )
    d_logs, d_quats, d_logit = pullback(tuple(arrived(2 + p) for p in range(4)))
    columns += list(d_logs) + list(d_quats) + [d_logit]
    turned = jnp.transpose(jnp.concatenate([asked] * 3, axis=0))
    hot_t = jnp.transpose(hot)
    for c in range(14):
        out_grad[c] = exact_dot(hot_t, columns[c], NN)
    basis = camera_basis([turned[c : c + 1, :] for c in range(6)])
    channel = lax.broadcasted_iota(jnp.int32, (3, 3 * devices), 1) // devices
    own_channel = channel == lax.broadcasted_iota(jnp.int32, (3, 3 * devices), 0)
    fan = jnp.concatenate([jnp.where(own_channel, value, 0.0) for value in basis], axis=0)
    hot_3 = jnp.transpose(jnp.concatenate([hot] * 3, axis=0))
    shades = fan.shape[0]
    routed = jnp.concatenate([hot_3 * fan[r : r + 1, :] for r in range(shades)], axis=0)
    tinted = jnp.concatenate([arrived(6 + ch) for ch in range(3)], axis=0)
    colour = jnp.dot(routed, tinted, precision=HIGHEST_MODE, preferred_element_type=F32)
    for r in range(shades):
        out_grad[14 + r] = colour[r * blocks : (r + 1) * blocks]
    losses = incoming_ref[:, ROW_REC * halves, :]
    out_loss[...] = jnp.sum(losses, axis=0, keepdims=True)[:, 0:1] * (
        1.0 / (devices * rows * cols)
    )
    fetch_one.wait()
    fetch_two.wait()
    comps = gauss_ref.shape[0]
    pieces = []
    for piece in range(PIECES):
        low, high = piece * comps // PIECES, (piece + 1) * comps // PIECES

        def update(c, carry):
            gradient = out_grad[c]
            new_one = 0.9 * one_v[c] + 0.1 * gradient
            new_two = 0.999 * two_v[c] + 0.001 * gradient * gradient
            one_v[c] = new_one
            two_v[c] = new_two
            bottom = jnp.sqrt(new_two * (1.0 / BIAS_SECOND)) + 1e-08
            gauss_v[c] = gauss_ref[c] - rates_ref[c] * new_one / bottom
            return carry

        lax.fori_loop(low, high, update, 0, unroll=2)
        part = pl.ds(low, high - low)
        for source, landing, sem in (
            (one_v, out_one, 0),
            (two_v, out_two, 1),
            (gauss_v, out_gauss, 2),
            (out_grad, out_grad_hbm, 3),
        ):
            copy = pltpu.make_async_copy(
                source.at[part], landing.at[part], write_sem.at[sem, piece]
            )
            copy.start()
            pieces.append(copy)
    for copy in pieces:
        copy.wait()


def per_device(
    gaussians,
    first_moment,
    second_moment,
    camera,
    target,
    block_list,
    block_count,
    tile_start,
    tile_end,
):
    views_n = lax.axis_size("view")
    bands_n = lax.axis_size("band")
    devices = views_n * bands_n
    blocks, comps, block_len = gaussians.shape
    list_len = block_list.shape[2]
    rows, cols = target.shape[2:]
    tiles = cols // TILE
    halves = block_len // 128
    geometry = (views_n, bands_n, blocks, list_len, rows, cols, block_len)

    across, first, second = smoothing_tables(rows, cols, 3)
    power = power_table(tiles, cols)
    vmem = pl.BlockSpec(memory_space=pltpu.VMEM)
    hbm = pl.BlockSpec(memory_space=pl.ANY)

    def by_comp(array):
        return jnp.transpose(array, (1, 0, 2))

    rec_rows = ROW_REC * halves
    window = TILE_MOST * block_len
    incoming, messages = pl.pallas_call(
        functools.partial(step_kernel, geometry),
        out_shape=(
            jax.ShapeDtypeStruct((devices, rec_rows + 1, 128), F32),
            jax.ShapeDtypeStruct((devices, 128), F32),
        ),
        in_specs=[vmem] * 5 + [hbm] + [vmem] * 4,
        out_specs=(vmem, vmem),
        scratch_shapes=[
            pltpu.VMEM((comps, blocks, block_len), F32),
            pltpu.VMEM((1, 128), F32),
            pltpu.VMEM((devices, 1, 128), F32),
            pltpu.VMEM((devices, GEO_REC * halves, 128), F32),
            pltpu.VMEM((devices, GEO_REC * halves, 128), F32),
            pltpu.VMEM((devices, rec_rows - GEO_REC * halves, 128), F32),
            pltpu.VMEM((devices, rec_rows - GEO_REC * halves, 128), F32),
            pltpu.VMEM((devices, rec_rows + 1, 128), F32),
            pltpu.VMEM((devices, rec_rows + 1, 128), F32),
            pltpu.VMEM((2, 3, REACH, cols), F32),
            pltpu.VMEM((2, 3, REACH, cols), F32),
            pltpu.VMEM((2, 3, REACH, cols), F32),
            pltpu.VMEM((2, 3, REACH, cols), F32),
            pltpu.VMEM((6, window, cols), F32),
            pltpu.VMEM((window, rows // 8, 8, cols), F32),
            pltpu.VMEM((window, rows // 8, 8, cols), F32),
            pltpu.VMEM((6, window, cols), F32),
            pltpu.SemaphoreType.DMA((4,)),
            pltpu.SemaphoreType.DMA((4,)),
            pltpu.SemaphoreType.DMA((2, 2)),
            pltpu.SemaphoreType.DMA((2, 2)),
            pltpu.SemaphoreType.DMA((1,)),
        ],
        compiler_params=pltpu.CompilerParams(collective_id=0, has_side_effects=True),
        name="render_step",
    )(
        camera,
        block_list,
        tile_start,
        tile_end,
        target,
        by_comp(gaussians),
        across,
        first,
        second,
        power,
    )

    rates = learning_rates() / BIAS_FIRST
    shape = jax.ShapeDtypeStruct((comps, blocks, block_len), F32)
    new_params, new_one, new_two, mean_loss, gradient = pl.pallas_call(
        functools.partial(adam_kernel, geometry),
        out_shape=(shape, shape, shape, jax.ShapeDtypeStruct((1, 1), F32), shape),
        in_specs=[vmem, vmem, pl.BlockSpec(memory_space=pltpu.SMEM), vmem, hbm, hbm],
        out_specs=(hbm, hbm, hbm, vmem, hbm),
        scratch_shapes=[pltpu.VMEM((comps, blocks, block_len), F32)] * 4
        + [pltpu.SemaphoreType.DMA((2,)), pltpu.SemaphoreType.DMA((4, PIECES))],
        name="adam_step",
    )(
        messages,
        incoming,
        rates,
        by_comp(gaussians),
        by_comp(first_moment),
        by_comp(second_moment),
    )
    return (
        by_comp(new_params),
        by_comp(new_one),
        by_comp(new_two),
        mean_loss.reshape(()),
        by_comp(gradient),
    )


def solution(mesh):
    return jax.shard_map(
        per_device,
        mesh=mesh,
        in_specs=(
            P(("view", "band"), None, None),
            P(("view", "band"), None, None),
            P(("view", "band"), None, None),
            P("view", None),
            P("view", None, "band", None),
            P("view", "band", None),
            P("view", "band"),
            P("view", "band", None),
            P("view", "band", None),
        ),
        out_specs=(
            P(("view", "band"), None, None),
            P(("view", "band"), None, None),
            P(("view", "band"), None, None),
            P(),
            P(("view", "band"), None, None),
        ),
        check_vma=False,
    )
```
